128 devices in a mesh: grid: 32 (over y, x, z_lo), ipts: 4 (over z_hi, core).
Axes of the slice: x: 4, y: 4, z: 4 (z_hi: 2, z_lo: 2; z = z_hi * 2 + z_lo), core: 2. Of those that a mesh axis runs over, the one named last changes fastest.
Arguments:
- orbitals: bfloat16 [65536, 1024], P(('grid', 'ipts')), may hold values from -1.1953125 to 1.1953125
- targets: bfloat16 [65536, 256], P(('grid', 'ipts')), may hold values from -6 to 6
- points: int32 [4, 4096], P('ipts', 'grid'), may hold values from 0 to 65535, as said below
- potential: bfloat16 [65536, 16384], P('grid', 'ipts'), may hold values from -0.046875 to 0.046875
Outputs:
- exchanged: bfloat16 [65536, 256], P(('grid', 'ipts'))
The draws below stay inside these ranges and needn't reach their ends.
Inputs may be any that keep to these rules, and one draw needn't show every extreme that they name: Indices are distinct over all groups; each row of points rises strictly, and its entries k * 128 to (k + 1) * 128 - 1 lie in grid rows k * 2048 to (k + 1) * 2048 - 1.
All inputs are finite; a program needn't handle non-finite values.
Results may differ from the reference program's by a relative error of at most 0.0049.
Values may be sent and summed in bfloat16 or wider, within the bound.
No kernel may reach another device: no remote copies, remote signals or barrier semaphores. Data moves between devices by JAX's collectives and lax.ppermute only.
A program may use at most 128 MiB of HBM per device.

```python
import jax
import jax.numpy as jnp
from jax import lax

NORB = 1024
NJ = 256
PTS_SLAB = 128
SLAB = 2048
GROUPS = 4
PER_GROUP = 4096
NG = 65536
NMU = 16384


def draw_points(key, part):
    slabs = PER_GROUP // PTS_SLAB
    keys = jax.random.split(jax.random.fold_in(key, 7), slabs)

    def one_slab(slab_key):
        order = jax.random.permutation(slab_key, SLAB)
        chosen = order[:GROUPS * PTS_SLAB].reshape(GROUPS, PTS_SLAB)
        return jnp.sort(chosen, axis=1).astype(jnp.int32)
    picks = jax.vmap(one_slab)(keys)
    offsets = (jnp.arange(slabs, dtype=jnp.int32) * SLAB)[:, None, None]
    return jnp.transpose(picks + offsets, (1, 0, 2)).reshape(GROUPS, PER_GROUP)


def steps_of(own_key, extent, cuts, low, top_value):
    gain = 1.0
    for position, parts in cuts:
        draws = jax.random.uniform(jax.random.fold_in(jax.random.fold_in(own_key, 6), position), (parts,), jnp.float32, low / len(cuts), top_value / len(cuts))
        gain = gain * jnp.repeat(jnp.exp(draws), extent[position] // parts).reshape((-1,) + (1,) * (len(extent) - 1 - position))
    return gain


def scatter_about(key, extent, deviation, bound, cuts=(), kind=jnp.bfloat16):
    factor_of = steps_of(key, extent, cuts, -0.22, 0.18) if cuts else 1.0
    values = jax.random.normal(key, extent, jnp.float32) * deviation * factor_of
    return jnp.minimum(jnp.maximum(values, -bound), bound).astype(kind)


def setup_inputs(seed: int = 0) -> dict:
    splits = jax.random.split(jax.random.key(seed), 5)
    orbitals = scatter_about(splits[0], (NG, NORB), 0.2, 1.1953125, ((0, 128),))
    targets = scatter_about(splits[1], (NG, NJ), 1.0, 6.0, ((0, 128),))
    points = draw_points(jax.random.fold_in(splits[4], 71), 0)
    potential = scatter_about(splits[3], (NG, NMU), (4 * PER_GROUP) ** -0.5, 0.046875, ((0, 32), (1, 4)))
    return dict(orbitals=orbitals, targets=targets, points=points, potential=potential)


def reference(orbitals, targets, points, potential):
    slabs = NG // SLAB
    values = []
    for group in range(GROUPS):
        index = points[group]
        values.append((jnp.take(orbitals, index, axis=0), jnp.take(targets, index, axis=0)))

    def one_slab(slab_index):
        start = slab_index * SLAB
        rows = lax.dynamic_slice_in_dim(orbitals, start, SLAB, 0)
        kernel_rows = lax.dynamic_slice_in_dim(potential, start, SLAB, 0)
        total = jnp.zeros((SLAB, NJ), jnp.float32)
        for group in range(GROUPS):
            orbital_values, target_values = values[group]
            products = lax.dot_general(rows, orbital_values, (((1,), (1,)), ((), ())), preferred_element_type=jnp.float32)
            kernel = kernel_rows[:, group * PER_GROUP:(group + 1) * PER_GROUP].astype(jnp.float32)
            weighted = (kernel * products).astype(jnp.bfloat16)
            total = total + jnp.dot(weighted, target_values, preferred_element_type=jnp.float32)
        return (-total).astype(jnp.bfloat16)

    result = lax.map(one_slab, jnp.arange(slabs, dtype=jnp.int32))
    return result.reshape(NG, NJ)
```

```python
import jax
import jax.numpy as jnp
from jax import lax
from jax.experimental import pallas as pl
from jax.experimental.pallas import tpu as pltpu
from jax.sharding import Mesh
from jax.sharding import PartitionSpec as P

AXES = ("y", "x", "zl", "zh", "c")
SLABS = ("y", "x", "zl")
IPTS = ("zh", "c")
RING = 4

ROUNDS = (
    (((0, 1), "x", 1), ((0, 3), "x", -1), ((1, 0), "y", 1), ((3, 0), "y", -1)),
    (((1, 1), "x", 1), ((3, 3), "x", -1), ((1, 3), "y", 1), ((3, 1), "y", -1)),
    (((0, 2), "x", 1), ((1, 2), "x", -1), ((2, 0), "y", 1), ((2, 1), "y", -1)),
    (((2, 2), "x", 1), ((3, 2), "x", -1), ((2, 3), "y", -1)),
)


def from_neighbour(value, axis, side):
    n = lax.axis_size(axis)
    return lax.ppermute(value, axis, [((i + side) % n, i) for i in range(n)])


def source_offset(block, axis, side):
    dy, dx = block
    return ((dy - side) % RING, dx) if axis == "y" else (dy, (dx - side) % RING)


def pick_kernel(bases, ids, own_orb, sib_orb, own_tgt, sib_tgt, mine, theirs):
    rows = own_orb.shape[0]
    norb = own_orb.shape[1]
    for k, out in ((0, mine), (1, theirs)):
        row = lax.broadcasted_iota(jnp.int32, (rows, out.shape[0]), 0)
        at = ids[k : k + 1, :]
        own = (row + bases[0] == at).astype(jnp.bfloat16)
        sib = (row + bases[1] == at).astype(jnp.bfloat16)
        dims = (((0,), (0,)), ((), ()))

        def select(hot, values):
            return lax.dot_general(hot, values, dims, preferred_element_type=jnp.float32)

        out[:, :norb] = (select(own, own_orb[...]) + select(sib, sib_orb[...])).astype(out.dtype)
        out[:, norb:] = (select(own, own_tgt[...]) + select(sib, sib_tgt[...])).astype(out.dtype)


def pick(bases, ids, own_orb, sib_orb, own_tgt, sib_tgt):
    points = ids.shape[1]
    width = own_orb.shape[1] + own_tgt.shape[1]
    out = jax.ShapeDtypeStruct((points, width), own_orb.dtype)
    whole = pl.BlockSpec(memory_space=pltpu.VMEM)
    return pl.pallas_call(
        pick_kernel,
        out_shape=(out, out),
        in_specs=[pl.BlockSpec(memory_space=pltpu.SMEM)] + [whole] * 5,
        out_specs=(whole, whole),
        compiler_params=pltpu.CompilerParams(vmem_limit_bytes=32 << 20),
        name="pick",
    )(bases, ids, own_orb, sib_orb, own_tgt, sib_tgt)


def apply_kernel(count, first, rows, cols, *refs):
    slab = refs[0]
    pairs = refs[1 : 1 + count]
    pots = refs[1 + count : 1 + 2 * count]
    out = refs[-1]
    norb = slab.shape[1]
    total = None if first else refs[1 + 2 * count][...]
    for pair, pot in zip(pairs, pots):
        products = lax.dot_general(
            slab[...], pair[:, :norb], (((1,), (1,)), ((), ())), preferred_element_type=jnp.float32
        )
        weighted = (pot[...].astype(jnp.float32) * products).astype(jnp.bfloat16)
        term = jnp.dot(weighted, pair[:, norb:], preferred_element_type=jnp.float32)
        total = term if total is None else total + term
    out[...] = total


def apply_pairs(slab, pairs, potential, rows, cols, total):
    count = len(pairs)
    tile = slab.shape[0] // 4
    norb = slab.shape[1]
    points, width = pairs[0].shape
    nj = width - norb
    acc = pl.BlockSpec((tile, nj), lambda i, r, c: (i, 0))

    def pot_spec(k):
        return pl.BlockSpec((tile, points), lambda i, r, c: (r[i], c[k]))

    first = total is None
    specs = [pl.BlockSpec((tile, norb), lambda i, r, c: (i, 0))]
    specs += [pl.BlockSpec((points, width), lambda i, r, c: (0, 0))] * count
    specs += [pot_spec(k) for k in range(count)]
    args = [slab, *pairs] + [potential] * count
    if not first:
        specs.append(acc)
        args.append(total)
    flops = 2 * slab.shape[0] * points * count * width
    moved = slab.size * 2 + count * (slab.shape[0] * points + points * width) * 2 + slab.shape[0] * nj * 8

    def body(r, c, *refs):
        apply_kernel(count, first, r, c, *refs)

    return pl.pallas_call(
        body,
        out_shape=jax.ShapeDtypeStruct((slab.shape[0], nj), jnp.float32),
        grid_spec=pltpu.PrefetchScalarGridSpec(
            num_scalar_prefetch=2, grid=(4,), in_specs=specs, out_specs=acc
        ),
        input_output_aliases={} if first else {len(args) + 1: 0},
        cost_estimate=pl.CostEstimate(flops=flops, bytes_accessed=moved, transcendentals=0),
        compiler_params=pltpu.CompilerParams(vmem_limit_bytes=40 << 20),
        name="apply",
    )(rows, cols, *args)


def after(value, *others):
    return lax.optimization_barrier((value, others))[0]


def local(orbitals, targets, points, potential):
    own_rows = orbitals.shape[0]
    zl, zh, c = (lax.axis_index(a) for a in ("zl", "zh", "c"))
    y, x = lax.axis_index("y"), lax.axis_index("x")
    slab_start = ((y * RING + x) * 2 + zl) * own_rows * 4

    sib_orb = from_neighbour(orbitals, "c", 1)
    sib_tgt = from_neighbour(targets, "c", 1)
    far_points = from_neighbour(points, "zh", 1)
    bases = jnp.stack([slab_start + (zh * 2 + c) * own_rows, slab_start + (zh * 2 + 1 - c) * own_rows])
    ids = jnp.concatenate([points, far_points], axis=0)
    mine, theirs = pick(bases.astype(jnp.int32), ids, orbitals, sib_orb, targets, sib_tgt)
    block = mine + from_neighbour(theirs, "zh", 1)
    near = from_neighbour(block, "zl", 1)
    low = jnp.where(zl == 0, block, near)
    high = jnp.where(zl == 0, near, block)
    pair = jnp.concatenate([low, high], axis=0)

    far_orb = from_neighbour(after(orbitals, near), "zh", 1)
    far_sib = from_neighbour(far_orb, "c", 1)
    slab = jnp.concatenate([orbitals, far_orb, sib_orb, far_sib], axis=0)
    rows = jnp.stack([zh * 2 + c, (1 - zh) * 2 + c, zh * 2 + 1 - c, (1 - zh) * 2 + 1 - c]).astype(jnp.int32)

    have = {(0, 0): pair}
    total = None
    pending = [(0, 0)]

    def columns(blocks):
        return jnp.stack([(y + dy) % RING * RING + (x + dx) % RING for dy, dx in blocks]).astype(jnp.int32)

    for moves in ROUNDS:
        new = {}
        for block_at, axis, side in moves:
            new[block_at] = from_neighbour(have[source_offset(block_at, axis, side)], axis, side)
        total = apply_pairs(slab, [have[k] for k in pending], potential, rows, columns(pending), total)
        have.update(new)
        pending = list(new)
    total = apply_pairs(slab, [have[k] for k in pending], potential, rows, columns(pending), total)

    half = 2 * own_rows
    both = total[:half] + from_neighbour(total[half:], "c", 1)
    away = from_neighbour(both[own_rows:].astype(jnp.bfloat16), "zh", 1)
    return (-(both[:own_rows] + away.astype(jnp.float32))).astype(jnp.bfloat16)


def solution(mesh):
    torus = Mesh(mesh.devices.reshape(RING, RING, 2, 2, 2), AXES)
    placed = (P(AXES, None), P(AXES, None), P(IPTS, SLABS), P(SLABS, IPTS))
    return jax.shard_map(local, mesh=torus, in_specs=placed, out_specs=P(AXES, None), check_vma=False)
```

```python
import jax
import jax.numpy as jnp
from jax import lax
from jax.experimental import pallas as pl
from jax.experimental.pallas import tpu as pltpu
from jax.sharding import Mesh
from jax.sharding import PartitionSpec as P

AXES = ("y", "x", "zl", "zh", "c")
SLABS = ("y", "x", "zl")
IPTS = ("zh", "c")
RING = 4
NEXT = (((0, 1), "x", 1), ((0, 3), "x", -1), ((1, 0), "y", 1), ((3, 0), "y", -1))


def take_from(value, axis, side):
    n = lax.axis_size(axis)
    return lax.ppermute(value, axis, [((i + side) % n, i) for i in range(n)])


def after(value, *others):
    return lax.optimization_barrier((value, others))[0]


def pick_kernel(bases, ids, orb, tgt, mine, theirs):
    rows, norb = orb.shape
    half = rows // 2
    for k, out in ((0, mine), (1, theirs)):
        row = lax.broadcasted_iota(jnp.int32, (rows, out.shape[0]), 0)
        row = row + jnp.where(row < half, bases[0], bases[1] - half)
        hot = (row == ids[k : k + 1, :]).astype(jnp.bfloat16)
        dims = (((0,), (0,)), ((), ()))
        out[:, :norb] = lax.dot_general(hot, orb[...], dims, preferred_element_type=jnp.float32).astype(out.dtype)
        out[:, norb:] = lax.dot_general(hot, tgt[...], dims, preferred_element_type=jnp.float32).astype(out.dtype)


def pick(bases, ids, orb, tgt):
    out = jax.ShapeDtypeStruct((ids.shape[1], orb.shape[1] + tgt.shape[1]), orb.dtype)
    whole = pl.BlockSpec(memory_space=pltpu.VMEM)
    return pl.pallas_call(
        pick_kernel,
        out_shape=(out, out),
        in_specs=[pl.BlockSpec(memory_space=pltpu.SMEM)] + [whole] * 3,
        out_specs=(whole, whole),
        compiler_params=pltpu.CompilerParams(vmem_limit_bytes=32 << 20),
        name="pick",
    )(bases, ids, orb, tgt)


def apply_parts(slab, parts, potential, rows, cols, total):
    count = len(cols)
    tile = slab.shape[0] // 2
    norb = slab.shape[1]
    points = sum(p.shape[0] for p in parts) // count
    width = parts[0].shape[1]
    nj = width - norb
    first = total is None

    def body(r, c, slab_ref, *refs):
        ours, pots, out = refs[: len(parts)], refs[len(parts) : len(parts) + count], refs[-1]
        here = pl.ds(pl.multiple_of(pl.program_id(0) * tile, tile), tile)
        orb = jnp.concatenate([p[:, :norb] for p in ours], axis=0)
        tgt = jnp.concatenate([p[:, norb:] for p in ours], axis=0)
        products = lax.dot_general(
            slab_ref[here, :], orb, (((1,), (1,)), ((), ())), preferred_element_type=jnp.float32
        )
        pot = jnp.concatenate([p[...] for p in pots], axis=1)
        weighted = (pot.astype(jnp.float32) * products).astype(jnp.bfloat16)
        term = jnp.dot(weighted, tgt, preferred_element_type=jnp.float32)
        out[here, :] = term if first else refs[len(parts) + count][here, :] + term

    def pot_spec(k):
        return pl.BlockSpec((tile, points), lambda i, r, c: (r[i], c[k]))

    whole = pl.BlockSpec(memory_space=pltpu.VMEM)
    specs = [whole] * (1 + len(parts)) + [pot_spec(k) for k in range(count)]
    args = [slab, *parts] + [potential] * count
    if not first:
        specs.append(whole)
        args.append(total)
    flops = 2 * slab.shape[0] * points * count * width
    return pl.pallas_call(
        body,
        out_shape=jax.ShapeDtypeStruct((slab.shape[0], nj), jnp.float32),
        grid_spec=pltpu.PrefetchScalarGridSpec(
            num_scalar_prefetch=2, grid=(2,), in_specs=specs, out_specs=whole
        ),
        input_output_aliases={} if first else {len(args) + 1: 0},
        cost_estimate=pl.CostEstimate(
            flops=flops, bytes_accessed=count * slab.shape[0] * points * 2, transcendentals=0
        ),
        compiler_params=pltpu.CompilerParams(vmem_limit_bytes=24 << 20),
        name="apply",
    )(rows, jnp.stack(cols).astype(jnp.int32), *args)


def local(orbitals, targets, points, potential):
    own_rows = orbitals.shape[0]
    potential = pltpu.with_memory_space_constraint(potential, pltpu.HBM)
    count = points.shape[1]
    y, x, zl, zh, c = (lax.axis_index(a) for a in AXES)
    slab_start = ((y * RING + x) * 2 + zl) * own_rows * 4

    sib_orb = take_from(orbitals, "c", 1)
    sib_tgt = take_from(targets, "c", 1)
    far_points = take_from(points, "zh", 1)
    near_slab = jnp.concatenate([orbitals, sib_orb], axis=0)
    near_tgt = jnp.concatenate([targets, sib_tgt], axis=0)
    near_rows = jnp.stack([zh * 2 + c, zh * 2 + 1 - c]).astype(jnp.int32)
    far_rows = jnp.stack([(1 - zh) * 2 + c, (1 - zh) * 2 + 1 - c]).astype(jnp.int32)
    ids = jnp.concatenate([points, far_points], axis=0)
    mine, theirs = pick((slab_start + near_rows * own_rows).astype(jnp.int32), ids, near_slab, near_tgt)
    block = mine + take_from(theirs, "zh", 1)

    def in_order(own, other):
        low, high = jnp.where(zl == 0, own, other), jnp.where(zl == 0, other, own)
        return jnp.concatenate([low, high], axis=0)

    def column(at):
        return (y + at[0]) % RING * RING + (x + at[1]) % RING

    def near_apply(parts, ats, total):
        return apply_parts(near_slab, parts, potential, near_rows, [column(at) for at in ats], total)

    def far_apply(parts, ats, total):
        return apply_parts(far_slab, parts, potential, far_rows, [column(at) for at in ats], total)

    own = {at: take_from(block, axis, side) for at, axis, side in NEXT}
    other = take_from(block, "zl", 1)
    others = {at: take_from(other, axis, side) for at, axis, side in NEXT}
    far_orb = take_from(after(orbitals, other, *own.values()), "zh", 1)
    pair = {at: in_order(own[at], others[at]) for at in own}
    pair[0, 0] = in_order(block, other)
    near = near_apply([pair[0, 0]], [(0, 0)], None)

    left, down, up, right = (after(pair[at], near) for at in ((3, 0), (0, 1), (1, 0), (0, 3)))
    own[0, 1], own[1, 0] = after(own[0, 1], near), after(own[1, 0], near)
    col = {(0, 2): take_from(own[0, 1], "x", 1), (2, 0): take_from(own[1, 0], "y", 1)}
    pair[3, 3] = take_from(left, "x", -1)
    pair[3, 1] = take_from(down, "y", -1)
    first = tuple(own)
    near = near_apply([pair[at] for at in first], first, near)
    pair[1, 1] = take_from(after(up, near, *col.values()), "x", 1)
    pair[1, 3] = take_from(after(right, near, *col.values()), "y", 1)
    for at in col:
        pair[at] = in_order(col[at], take_from(after(col[at], near), "zl", 1))
    far_sib = take_from(after(far_orb, pair[3, 3]), "c", 1)
    far_slab = jnp.concatenate([far_orb, far_sib], axis=0)
    pair[3, 2] = take_from(pair[3, 3], "x", -1)
    pair[2, 1] = take_from(pair[3, 1], "y", -1)
    far = far_apply([pair[0, 0]] + [pair[at] for at in first], ((0, 0),) + first, None)

    pair[2, 3] = take_from(after(pair[1, 3], far), "y", 1)
    edge = take_from(after(pair[1, 1][:count], far), "x", 1)
    second = ((3, 3), (3, 1), (1, 1), (1, 3))
    near = near_apply([pair[at] for at in second], second, near)

    edge = [edge, take_from(after(pair[1, 3][count:], near), "x", -1)]
    corner = [
        take_from(after(pair[2, 1][:count], near), "x", 1),
        take_from(after(pair[3, 2][count:], near), "y", -1),
    ]
    far = far_apply([pair[at] for at in second], second, far)
    third = ((0, 2), (2, 0), (3, 2), (2, 1))
    near = near_apply([pair[at] for at in third], third, after(near, far))
    far = far_apply([pair[at] for at in third], third, after(far, near))
    last = [pair[2, 3], *edge, *corner]
    ats = ((2, 3), (1, 2), (2, 2))
    far = far_apply(last, ats, far)
    near = near_apply(last, ats, after(near, far))

    far = far[:own_rows] + take_from(far[own_rows:], "c", 1)
    away = take_from(far.astype(jnp.bfloat16), "zh", 1)
    near = near[:own_rows] + take_from(near[own_rows:], "c", 1)
    return (-(near + away.astype(jnp.float32))).astype(jnp.bfloat16)


def solution(mesh):
    torus = Mesh(mesh.devices.reshape(RING, RING, 2, 2, 2), AXES)
    placed = (P(AXES, None), P(AXES, None), P(IPTS, SLABS), P(SLABS, IPTS))
    return jax.shard_map(local, mesh=torus, in_specs=placed, out_specs=P(AXES, None), check_vma=False)
```

```python
import jax
import jax.numpy as jnp
from jax import lax
from jax.experimental import pallas as pl
from jax.experimental.pallas import tpu as pltpu
from jax.sharding import Mesh
from jax.sharding import PartitionSpec as P

AXES = ("y", "x", "zl", "zh", "c")
SLABS = ("y", "x", "zl")
IPTS = ("zh", "c")
RING = 4
NEXT = (((0, 1), "x", 1), ((0, 3), "x", -1), ((1, 0), "y", 1), ((3, 0), "y", -1))


def take_from(value, axis, side):
    n = lax.axis_size(axis)
    return lax.ppermute(value, axis, [((i + side) % n, i) for i in range(n)])


def after(value, *others):
    return lax.optimization_barrier((value, others))[0]


def pick_kernel(bases, ids, orb, tgt, mine, theirs):
    rows, norb = orb.shape
    half = rows // 2
    for k, out in ((0, mine), (1, theirs)):
        row = lax.broadcasted_iota(jnp.int32, (rows, out.shape[0]), 0)
        row = row + jnp.where(row < half, bases[0], bases[1] - half)
        hot = (row == ids[k : k + 1, :]).astype(jnp.bfloat16)
        dims = (((0,), (0,)), ((), ()))
        out[:, :norb] = lax.dot_general(hot, orb[...], dims, preferred_element_type=jnp.float32).astype(out.dtype)
        out[:, norb:] = lax.dot_general(hot, tgt[...], dims, preferred_element_type=jnp.float32).astype(out.dtype)


def pick(bases, ids, orb, tgt):
    out = jax.ShapeDtypeStruct((ids.shape[1], orb.shape[1] + tgt.shape[1]), orb.dtype)
    whole = pl.BlockSpec(memory_space=pltpu.VMEM)
    return pl.pallas_call(
        pick_kernel,
        out_shape=(out, out),
        in_specs=[pl.BlockSpec(memory_space=pltpu.SMEM)] + [whole] * 3,
        out_specs=(whole, whole),
        compiler_params=pltpu.CompilerParams(vmem_limit_bytes=32 << 20),
        name="pick",
    )(bases, ids, orb, tgt)


def apply_parts(slab, parts, potential, rows, cols, total, last=False):
    count = len(cols)
    tile = slab.shape[0] // 2
    norb = slab.shape[1]
    points = sum(p.shape[0] for p in parts) // count
    width = parts[0].shape[1]
    nj = width - norb
    first = total is None

    def body(r, c, slab_ref, *refs):
        ours, pots = refs[: len(parts)], refs[len(parts) : len(parts) + count]
        here = pl.ds(pl.multiple_of(pl.program_id(0) * tile, tile), tile)
        orb = jnp.concatenate([p[:, :norb] for p in ours], axis=0)
        tgt = jnp.concatenate([p[:, norb:] for p in ours], axis=0)
        products = lax.dot_general(
            slab_ref[here, :], orb, (((1,), (1,)), ((), ())), preferred_element_type=jnp.float32
        )
        pot = jnp.concatenate([p[...] for p in pots], axis=1)
        weighted = (pot.astype(jnp.float32) * products).astype(jnp.bfloat16)
        term = jnp.dot(weighted, tgt, preferred_element_type=jnp.float32)
        if not first:
            term = refs[len(parts) + count][here, :] + term
        if not last:
            refs[-1][here, :] = term
            return
        for k, out in enumerate(refs[-2:]):

            @pl.when(pl.program_id(0) == k)
            def _():
                out[...] = term

    def pot_spec(k):
        return pl.BlockSpec((tile, points), lambda i, r, c: (r[i], c[k]))

    whole = pl.BlockSpec(memory_space=pltpu.VMEM)
    fixed = [pl.BlockSpec(p.shape, lambda i, r, c: (0, 0)) for p in parts] if last else [whole] * len(parts)
    specs = [whole, *fixed] + [pot_spec(k) for k in range(count)]
    args = [slab, *parts] + [potential] * count
    if not first:
        specs.append(whole)
        args.append(total)
    flops = 2 * slab.shape[0] * points * count * width
    half = jax.ShapeDtypeStruct((tile, nj), jnp.float32)
    out_spec = pl.BlockSpec((tile, nj), lambda i, r, c: (0, 0))
    return pl.pallas_call(
        body,
        out_shape=(half, half) if last else jax.ShapeDtypeStruct((slab.shape[0], nj), jnp.float32),
        grid_spec=pltpu.PrefetchScalarGridSpec(
            num_scalar_prefetch=2, grid=(2,), in_specs=specs, out_specs=(out_spec,) * 2 if last else whole
        ),
        input_output_aliases={} if first or last else {len(args) + 1: 0},
        cost_estimate=pl.CostEstimate(
            flops=flops, bytes_accessed=count * slab.shape[0] * points * 2, transcendentals=0
        ),
        compiler_params=pltpu.CompilerParams(vmem_limit_bytes=15 << 20),
        name="apply",
    )(rows, jnp.stack(cols).astype(jnp.int32), *args)


def local(orbitals, targets, points, potential):
    own_rows = orbitals.shape[0]
    potential = pltpu.with_memory_space_constraint(potential, pltpu.HBM)
    count = points.shape[1]
    y, x, zl, zh, c = (lax.axis_index(a) for a in AXES)
    slab_start = ((y * RING + x) * 2 + zl) * own_rows * 4

    sib_orb = take_from(orbitals, "c", 1)
    sib_tgt = take_from(targets, "c", 1)
    far_points = take_from(points, "zh", 1)
    near_slab = jnp.concatenate([orbitals, sib_orb], axis=0)
    near_tgt = jnp.concatenate([targets, sib_tgt], axis=0)
    near_rows = jnp.stack([zh * 2 + c, zh * 2 + 1 - c]).astype(jnp.int32)
    far_rows = jnp.stack([(1 - zh) * 2 + c, (1 - zh) * 2 + 1 - c]).astype(jnp.int32)
    ids = jnp.concatenate([points, far_points], axis=0)
    mine, theirs = pick((slab_start + near_rows * own_rows).astype(jnp.int32), ids, near_slab, near_tgt)
    block = mine + take_from(theirs, "zh", 1)

    def in_order(own, other):
        low, high = jnp.where(zl == 0, own, other), jnp.where(zl == 0, other, own)
        return jnp.concatenate([low, high], axis=0)

    def column(at):
        return (y + at[0]) % RING * RING + (x + at[1]) % RING

    def near_apply(parts, ats, total, last=False):
        return apply_parts(near_slab, parts, potential, near_rows, [column(at) for at in ats], total, last)

    def far_apply(parts, ats, total, last=False):
        return apply_parts(far_slab, parts, potential, far_rows, [column(at) for at in ats], total, last)

    own = {at: take_from(block, axis, side) for at, axis, side in NEXT}
    other = take_from(block, "zl", 1)
    far_orb = take_from(after(orbitals, other), "zh", 1)
    others = {at: take_from(other, axis, side) for at, axis, side in NEXT}
    pair = {at: in_order(own[at], others[at]) for at in own}
    pair[0, 0] = in_order(block, other)
    near = near_apply([pair[0, 0]], [(0, 0)], None)

    def joined(whole, half):
        return jnp.concatenate([pair[whole], half], axis=0)

    from_right = take_from(joined((1, 0), pair[0, 1][:count]), "x", 1)
    from_left = take_from(joined((3, 0), pair[0, 3][count:]), "x", -1)
    from_up = take_from(joined((0, 3), pair[1, 0][:count]), "y", 1)
    from_down = take_from(joined((0, 1), pair[3, 0][count:]), "y", -1)
    first = tuple(at for at, _, _ in NEXT)
    far_sib = take_from(far_orb, "c", 1)
    far_slab = jnp.concatenate([far_orb, far_sib], axis=0)
    near = near_apply([pair[at] for at in first], first, near)
    far = far_apply([pair[0, 0]] + [pair[at] for at in first], ((0, 0),) + first, None)
    both = 2 * count
    pair[1, 1], pair[3, 3] = from_right[:both], from_left[:both]
    pair[1, 3], pair[3, 1] = from_up[:both], from_down[:both]
    pair[0, 2] = jnp.concatenate([from_right[both:], from_left[both:]], axis=0)
    pair[2, 0] = jnp.concatenate([from_up[both:], from_down[both:]], axis=0)

    low, high = after(pair[1, 1], near, far), after(pair[3, 3], near, far)
    pair[1, 2] = take_from(low, "x", 1)
    pair[3, 2] = take_from(high, "x", -1)
    pair[2, 1] = take_from(low, "y", 1)
    pair[2, 3] = take_from(high, "y", -1)
    second = ((1, 1), (3, 3), (1, 3), (3, 1), (0, 2), (2, 0))
    far = far_apply([pair[at] for at in second], second, far)
    near = near_apply([pair[at] for at in second], second, after(near, far))

    third = ((1, 2), (3, 2), (2, 1), (2, 3))
    part = both // 4
    sides = (((2, 1), "x", 1), ((2, 3), "x", -1), ((1, 2), "y", 1), ((3, 2), "y", -1))
    last = [
        take_from(after(pair[at][k * part : (k + 1) * part], near, far), axis, side)
        for k, (at, axis, side) in enumerate(sides)
    ]
    far = far_apply([pair[at] for at in third], third, far)
    kept, sent = far_apply(last, [(2, 2)], far, True)
    far = (kept + take_from(sent, "c", 1)).astype(jnp.bfloat16)
    away = take_from(far, "zh", 1)
    kept, sent = near_apply([pair[at] for at in third] + last, third + ((2, 2),), after(near, far), True)
    near = kept + take_from(after(sent, away), "c", 1)
    return (-(near + away.astype(jnp.float32))).astype(jnp.bfloat16)


def solution(mesh):
    torus = Mesh(mesh.devices.reshape(RING, RING, 2, 2, 2), AXES)
    placed = (P(AXES, None), P(AXES, None), P(IPTS, SLABS), P(SLABS, IPTS))
    return jax.shard_map(local, mesh=torus, in_specs=placed, out_specs=P(AXES, None), check_vma=False)
```

```python
import jax
import jax.numpy as jnp
from jax import lax
from jax.experimental import pallas as pl
from jax.experimental.pallas import tpu as pltpu
from jax.sharding import Mesh
from jax.sharding import PartitionSpec as P

AXES = ("y", "x", "zl", "zh", "c")
SLABS = ("y", "x", "zl")
IPTS = ("zh", "c")
RING = 4
ORDER = (
    (0, 0), (0, 1), (0, 3), (1, 0), (3, 0), (1, 1), (3, 3), (1, 3), (3, 1), (0, 2), (2, 0),
    (1, 2), (3, 2), (2, 1), (2, 3), (2, 2),
)
NEAR, FAR, BASE, SIDE = 16, 18, 20, 21
NEXT = (((0, 1), "x", 1), ((0, 3), "x", -1), ((1, 0), "y", 1), ((3, 0), "y", -1))


def take_from(value, axis, side):
    n = lax.axis_size(axis)
    return lax.ppermute(value, axis, [((i + side) % n, i) for i in range(n)])


def after(value, *others):
    return lax.optimization_barrier((value, others))[0]


def pick_kernel(table, ids, orb, tgt, mine, theirs):
    rows, norb = orb.shape
    half = rows // 2
    bases = [table[BASE] + table[NEAR + k] * half for k in range(2)]
    for k, out in ((0, mine), (1, theirs)):
        row = lax.broadcasted_iota(jnp.int32, (rows, out.shape[0]), 0)
        row = row + jnp.where(row < half, bases[0], bases[1] - half)
        hot = (row == ids[k : k + 1, :]).astype(jnp.bfloat16)
        dims = (((0,), (0,)), ((), ()))
        out[:, :norb] = lax.dot_general(hot, orb[...], dims, preferred_element_type=jnp.float32).astype(out.dtype)
        out[:, norb:] = lax.dot_general(hot, tgt[...], dims, preferred_element_type=jnp.float32).astype(out.dtype)


def pick(table, ids, orb, tgt):
    out = jax.ShapeDtypeStruct((ids.shape[1], orb.shape[1] + tgt.shape[1]), orb.dtype)
    whole = pl.BlockSpec(memory_space=pltpu.VMEM)
    return pl.pallas_call(
        pick_kernel,
        out_shape=(out, out),
        in_specs=[pl.BlockSpec(memory_space=pltpu.SMEM)] + [whole] * 3,
        out_specs=(whole, whole),
        compiler_params=pltpu.CompilerParams(vmem_limit_bytes=32 << 20),
        name="pick",
    )(table, ids, orb, tgt)


def apply_parts(slab, parts, potential, table, row_at, col_at, count, total, last=False):
    tile = slab.shape[0] // 2
    norb = slab.shape[1]
    points = sum(p.shape[0] for p in parts) // count
    width = parts[0].shape[1]
    nj = width - norb
    first = total is None

    def body(t, slab_ref, *refs):
        ours, pots = refs[: len(parts)], refs[len(parts) : len(parts) + count]
        here = pl.ds(pl.multiple_of(pl.program_id(0) * tile, tile), tile)
        orb = jnp.concatenate([p[:, :norb] for p in ours], axis=0)
        tgt = jnp.concatenate([p[:, norb:] for p in ours], axis=0)
        products = lax.dot_general(
            slab_ref[here, :], orb, (((1,), (1,)), ((), ())), preferred_element_type=jnp.float32
        )
        pot = jnp.concatenate([p[...] for p in pots], axis=1)
        weighted = (pot.astype(jnp.float32) * products).astype(jnp.bfloat16)
        term = jnp.dot(weighted, tgt, preferred_element_type=jnp.float32)
        if not first:
            term = refs[len(parts) + count][here, :] + term
        if not last:
            refs[-1][here, :] = term
            return
        for k, out in enumerate(refs[-2:]):

            @pl.when(pl.program_id(0) == k)
            def _():
                out[...] = term

    def pot_spec(k):
        return pl.BlockSpec((tile, points), lambda i, t: (t[row_at + i], t[col_at + k]))

    whole = pl.BlockSpec(memory_space=pltpu.VMEM)
    specs = [whole] * (1 + len(parts)) + [pot_spec(k) for k in range(count)]
    args = [slab, *parts] + [potential] * count
    if not first:
        specs.append(whole)
        args.append(total)
    flops = slab.shape[0] * points * count * width // 2
    half = jax.ShapeDtypeStruct((tile, nj), jnp.float32)
    return pl.pallas_call(
        body,
        out_shape=(half, half) if last else jax.ShapeDtypeStruct((slab.shape[0], nj), jnp.float32),
        grid_spec=pltpu.PrefetchScalarGridSpec(
            num_scalar_prefetch=1, grid=(2,), in_specs=specs, out_specs=(whole,) * 2 if last else whole
        ),
        input_output_aliases={} if first or last else {len(args): 0},
        cost_estimate=pl.CostEstimate(
            flops=flops, bytes_accessed=count * slab.shape[0] * points * 2, transcendentals=0
        ),
        compiler_params=pltpu.CompilerParams(vmem_limit_bytes=15 << 20),
        name="apply",
    )(table, *args)


def local(orbitals, targets, points, potential):
    own_rows = orbitals.shape[0]
    potential = pltpu.with_memory_space_constraint(potential, pltpu.HBM)
    count = points.shape[1]
    y, x, zl, zh, c = (lax.axis_index(a) for a in AXES)
    slab_start = ((y * RING + x) * 2 + zl) * own_rows * 4

    n = lax.iota(jnp.int32, SIDE + 1)
    code = jnp.zeros_like(n)
    for k, (dy, dx) in enumerate(ORDER):
        code = jnp.where(n == k, dy * RING + dx, code)
    cols = (y + code // RING) % RING * RING + (x + code % RING) % RING
    half_at = jnp.where(n < FAR, zh, 1 - zh)
    rows = half_at * 2 + jnp.where((n - NEAR) % 2 == 0, c, 1 - c)
    table = jnp.where(n < NEAR, cols, jnp.where(n < BASE, rows, jnp.where(n < SIDE, slab_start, zl)))
    table = table.astype(jnp.int32)

    sib_orb = take_from(orbitals, "c", 1)
    sib_tgt = take_from(targets, "c", 1)
    far_points = take_from(points, "zh", 1)
    near_slab = jnp.concatenate([orbitals, sib_orb], axis=0)
    near_tgt = jnp.concatenate([targets, sib_tgt], axis=0)
    ids = jnp.concatenate([points, far_points], axis=0)
    mine, theirs = pick(table, ids, near_slab, near_tgt)
    block = mine + take_from(theirs, "zh", 1)

    def near_apply(parts, ats, total, last=False):
        return apply_parts(near_slab, parts, potential, table, NEAR, ORDER.index(ats[0]), len(ats), total, last)

    def far_apply(parts, ats, total, last=False):
        return apply_parts(far_slab, parts, potential, table, FAR, ORDER.index(ats[0]), len(ats), total, last)

    other = take_from(block, "zl", 1)
    lower = table[SIDE:].reshape(1, 1) == 0
    low, high = jnp.where(lower, block, other), jnp.where(lower, other, block)
    pair = {(0, 0): jnp.concatenate([low, high], axis=0)}
    far_orb = take_from(after(orbitals, other), "zh", 1)
    for at, axis, side in NEXT:
        pair[at] = take_from(pair[0, 0], axis, side)
    near = near_apply([pair[0, 0]], [(0, 0)], None)

    def joined(whole, half):
        return jnp.concatenate([pair[whole], half], axis=0)

    from_right = take_from(joined((1, 0), pair[0, 1][:count]), "x", 1)
    from_left = take_from(joined((3, 0), pair[0, 3][count:]), "x", -1)
    from_up = take_from(joined((0, 3), pair[1, 0][:count]), "y", 1)
    from_down = take_from(joined((0, 1), pair[3, 0][count:]), "y", -1)
    first = tuple(at for at, _, _ in NEXT)
    near = near_apply([pair[at] for at in first], first, near)
    far_sib = take_from(far_orb, "c", 1)
    far_slab = jnp.concatenate([far_orb, far_sib], axis=0)
    far = far_apply([pair[0, 0]] + [pair[at] for at in first], ((0, 0),) + first, None)
    from_right, from_left, from_up, from_down = lax.optimization_barrier(
        (from_right, from_left, from_up, from_down, near, far)
    )[:4]
    both = 2 * count
    pair[1, 1], pair[3, 3] = from_right[:both], from_left[:both]
    pair[1, 3], pair[3, 1] = from_up[:both], from_down[:both]
    pair[0, 2] = jnp.concatenate([from_right[both:], from_left[both:]], axis=0)
    pair[2, 0] = jnp.concatenate([from_up[both:], from_down[both:]], axis=0)

    pair[1, 2] = take_from(pair[1, 1], "x", 1)
    pair[3, 2] = take_from(pair[3, 3], "x", -1)
    pair[2, 1] = take_from(pair[1, 1], "y", 1)
    pair[2, 3] = take_from(pair[3, 3], "y", -1)
    second = ((1, 1), (3, 3), (1, 3), (3, 1), (0, 2), (2, 0))
    far = far_apply([pair[at] for at in second], second, far)
    near = near_apply([pair[at] for at in second], second, after(near, far))

    third = ((1, 2), (3, 2), (2, 1), (2, 3))
    ready = lax.optimization_barrier((*(pair[at] for at in third), near, far))[:4]
    pair.update(zip(third, ready))
    part = both // 4
    sides = (((2, 1), "x", 1), ((2, 3), "x", -1), ((1, 2), "y", 1), ((3, 2), "y", -1))
    last = [
        take_from(pair[at][k * part : (k + 1) * part], axis, side)
        for k, (at, axis, side) in enumerate(sides)
    ]
    far = far_apply([pair[at] for at in third], third, far)
    kept, sent = far_apply(last, [(2, 2)], far, True)
    far = (kept + take_from(sent, "c", 1)).astype(jnp.bfloat16)
    away = take_from(far, "zh", 1)
    kept, sent = near_apply([pair[at] for at in third] + last, third + ((2, 2),), after(near, far), True)
    near = kept + take_from(after(sent, away), "c", 1)
    return (-(near + away.astype(jnp.float32))).astype(jnp.bfloat16)


def solution(mesh):
    torus = Mesh(mesh.devices.reshape(RING, RING, 2, 2, 2), AXES)
    placed = (P(AXES, None), P(AXES, None), P(IPTS, SLABS), P(SLABS, IPTS))
    return jax.shard_map(local, mesh=torus, in_specs=placed, out_specs=P(AXES, None), check_vma=False)
```

```python
import jax
import jax.numpy as jnp
from jax import lax
from jax.experimental import pallas as pl
from jax.experimental.pallas import tpu as pltpu
from jax.sharding import Mesh
from jax.sharding import PartitionSpec as P

AXES = ("y", "x", "zl", "zh", "c")
SLABS = ("y", "x", "zl")
IPTS = ("zh", "c")
RING = 4
ORDER = (
    (0, 0), (0, 1), (0, 3), (1, 0), (3, 0), (1, 1), (3, 3), (1, 3), (3, 1), (0, 2), (2, 0),
    (1, 2), (3, 2), (2, 1), (2, 3), (2, 2),
)
NEAR, FAR, BASE, SIDE = 16, 18, 20, 21
NEXT = (((0, 1), "x", 1), ((0, 3), "x", -1), ((1, 0), "y", 1), ((3, 0), "y", -1))


def take_from(value, axis, side):
    n = lax.axis_size(axis)
    return lax.ppermute(value, axis, [((i + side) % n, i) for i in range(n)])


def after(value, *others):
    return lax.optimization_barrier((value, others))[0]


def pick_kernel(table, ids, orb, tgt, mine, theirs):
    rows, norb = orb.shape
    half = rows // 2
    bases = [table[BASE] + table[NEAR + k] * half for k in range(2)]
    for k, out in ((0, mine), (1, theirs)):
        row = lax.broadcasted_iota(jnp.int32, (rows, out.shape[0]), 0)
        row = row + jnp.where(row < half, bases[0], bases[1] - half)
        hot = (row == ids[k : k + 1, :]).astype(jnp.bfloat16)
        dims = (((0,), (0,)), ((), ()))
        out[:, :norb] = lax.dot_general(hot, orb[...], dims, preferred_element_type=jnp.float32).astype(out.dtype)
        out[:, norb:] = lax.dot_general(hot, tgt[...], dims, preferred_element_type=jnp.float32).astype(out.dtype)


def pick(table, ids, orb, tgt):
    out = jax.ShapeDtypeStruct((ids.shape[1], orb.shape[1] + tgt.shape[1]), orb.dtype)
    whole = pl.BlockSpec(memory_space=pltpu.VMEM)
    return pl.pallas_call(
        pick_kernel,
        out_shape=(out, out),
        in_specs=[pl.BlockSpec(memory_space=pltpu.SMEM)] + [whole] * 3,
        out_specs=(whole, whole),
        compiler_params=pltpu.CompilerParams(vmem_limit_bytes=32 << 20),
        name="pick",
    )(table, ids, orb, tgt)


def apply_parts(slab, parts, potential, table, row_at, col_at, count, total, last=False):
    tile = slab.shape[0] // 2
    norb = slab.shape[1]
    points = sum(p.shape[0] for p in parts) // count
    width = parts[0].shape[1]
    nj = width - norb
    first = total is None

    def body(t, slab_ref, *refs):
        ours, pots = refs[: len(parts)], refs[len(parts) : len(parts) + count]
        here = pl.ds(pl.multiple_of(pl.program_id(0) * tile, tile), tile)
        orb = jnp.concatenate([p[:, :norb] for p in ours], axis=0)
        tgt = jnp.concatenate([p[:, norb:] for p in ours], axis=0)
        products = lax.dot_general(
            slab_ref[here, :], orb, (((1,), (1,)), ((), ())), preferred_element_type=jnp.float32
        )
        pot = jnp.concatenate([p[...] for p in pots], axis=1)
        weighted = (pot.astype(jnp.float32) * products).astype(jnp.bfloat16)
        term = jnp.dot(weighted, tgt, preferred_element_type=jnp.float32)
        if not first:
            term = refs[len(parts) + count][here, :] + term
        if not last:
            refs[-1][here, :] = term
            return
        for k, out in enumerate(refs[-2:]):

            @pl.when(pl.program_id(0) == k)
            def _():
                out[...] = term

    def pot_spec(k):
        return pl.BlockSpec((tile, points), lambda i, t: (t[row_at + i], t[col_at + k]))

    whole = pl.BlockSpec(memory_space=pltpu.VMEM)
    specs = [whole] * (1 + len(parts)) + [pot_spec(k) for k in range(count)]
    args = [slab, *parts] + [potential] * count
    if not first:
        specs.append(whole)
        args.append(total)
    flops = slab.shape[0] * points * count * width // 2
    half = jax.ShapeDtypeStruct((tile, nj), jnp.float32)
    return pl.pallas_call(
        body,
        out_shape=(half, half) if last else jax.ShapeDtypeStruct((slab.shape[0], nj), jnp.float32),
        grid_spec=pltpu.PrefetchScalarGridSpec(
            num_scalar_prefetch=1, grid=(2,), in_specs=specs, out_specs=(whole,) * 2 if last else whole
        ),
        input_output_aliases={} if first or last else {len(args): 0},
        cost_estimate=pl.CostEstimate(
            flops=flops, bytes_accessed=count * slab.shape[0] * points * 2, transcendentals=0
        ),
        compiler_params=pltpu.CompilerParams(vmem_limit_bytes=15 << 20),
        name="apply",
    )(table, *args)


def local(orbitals, targets, points, potential):
    own_rows = orbitals.shape[0]
    potential = pltpu.with_memory_space_constraint(potential, pltpu.HBM)
    count = points.shape[1]
    y, x, zl, zh, c = (lax.axis_index(a) for a in AXES)
    slab_start = ((y * RING + x) * 2 + zl) * own_rows * 4

    n = lax.iota(jnp.int32, SIDE + 1)
    code = jnp.zeros_like(n)
    for k, (dy, dx) in enumerate(ORDER):
        code = jnp.where(n == k, dy * RING + dx, code)
    cols = (y + code // RING) % RING * RING + (x + code % RING) % RING
    half_at = jnp.where(n < FAR, zh, 1 - zh)
    rows = half_at * 2 + jnp.where((n - NEAR) % 2 == 0, c, 1 - c)
    table = jnp.where(n < NEAR, cols, jnp.where(n < BASE, rows, jnp.where(n < SIDE, slab_start, zl)))
    table = table.astype(jnp.int32)

    sib_orb = take_from(orbitals, "c", 1)
    sib_tgt = take_from(targets, "c", 1)
    far_points = take_from(points, "zh", 1)
    near_slab = jnp.concatenate([orbitals, sib_orb], axis=0)
    near_tgt = jnp.concatenate([targets, sib_tgt], axis=0)
    ids = jnp.concatenate([points, far_points], axis=0)
    mine, theirs = pick(table, ids, near_slab, near_tgt)
    early = own_rows * 3 // 8
    far_early = take_from(orbitals[:early], "zh", 1)
    block = mine + take_from(after(theirs, far_early), "zh", 1)

    def near_apply(parts, ats, total, last=False):
        return apply_parts(near_slab, parts, potential, table, NEAR, ORDER.index(ats[0]), len(ats), total, last)

    def far_apply(parts, ats, total, last=False):
        return apply_parts(far_slab, parts, potential, table, FAR, ORDER.index(ats[0]), len(ats), total, last)

    other = take_from(block, "zl", 1)
    lower = table[SIDE:].reshape(1, 1) == 0
    low, high = jnp.where(lower, block, other), jnp.where(lower, other, block)
    pair = {(0, 0): jnp.concatenate([low, high], axis=0)}
    far_late = take_from(after(orbitals[early:], other), "zh", 1)
    for at, axis, side in NEXT:
        pair[at] = take_from(pair[0, 0], axis, side)
    far_orb = jnp.concatenate([far_early, far_late], axis=0)

    def joined(whole, half):
        return jnp.concatenate([pair[whole], half], axis=0)

    from_right = take_from(joined((1, 0), pair[0, 1][:count]), "x", 1)
    from_left = take_from(joined((3, 0), pair[0, 3][count:]), "x", -1)
    from_up = take_from(joined((0, 3), pair[1, 0][:count]), "y", 1)
    from_down = take_from(joined((0, 1), pair[3, 0][count:]), "y", -1)
    first = tuple(at for at, _, _ in NEXT)
    near = near_apply([pair[0, 0]] + [pair[at] for at in first], ((0, 0),) + first, None)
    far_sib = take_from(far_orb, "c", 1)
    far_slab = jnp.concatenate([far_orb, far_sib], axis=0)
    far = far_apply([pair[0, 0]] + [pair[at] for at in first], ((0, 0),) + first, None)
    from_right, from_left, from_up, from_down = lax.optimization_barrier(
        (from_right, from_left, from_up, from_down, near, far)
    )[:4]
    both = 2 * count
    pair[1, 1], pair[3, 3] = from_right[:both], from_left[:both]
    pair[1, 3], pair[3, 1] = from_up[:both], from_down[:both]
    pair[0, 2] = jnp.concatenate([from_right[both:], from_left[both:]], axis=0)
    pair[2, 0] = jnp.concatenate([from_up[both:], from_down[both:]], axis=0)

    pair[1, 2] = take_from(pair[1, 1], "x", 1)
    pair[3, 2] = take_from(pair[3, 3], "x", -1)
    pair[2, 1] = take_from(pair[1, 1], "y", 1)
    pair[2, 3] = take_from(pair[3, 3], "y", -1)
    second = ((1, 1), (3, 3), (1, 3), (3, 1), (0, 2), (2, 0))
    far = far_apply([pair[at] for at in second], second, far)
    near = near_apply([pair[at] for at in second], second, after(near, far))

    third = ((1, 2), (3, 2), (2, 1), (2, 3))
    ready = lax.optimization_barrier((*(pair[at] for at in third), near, far))[:4]
    pair.update(zip(third, ready))
    last = [take_from(pair[2, 1][:count], "x", 1), take_from(pair[1, 2][count:], "y", 1)]
    far = far_apply([pair[at] for at in third], third, far)
    kept, sent = far_apply(last, [(2, 2)], far, True)
    far = (kept + take_from(sent, "c", 1)).astype(jnp.bfloat16)
    away = take_from(far, "zh", 1)
    kept, sent = near_apply([pair[at] for at in third] + last, third + ((2, 2),), after(near, far), True)
    near = kept + take_from(after(sent, away), "c", 1)
    return (-(near + away.astype(jnp.float32))).astype(jnp.bfloat16)


def solution(mesh):
    torus = Mesh(mesh.devices.reshape(RING, RING, 2, 2, 2), AXES)
    placed = (P(AXES, None), P(AXES, None), P(IPTS, SLABS), P(SLABS, IPTS))
    return jax.shard_map(local, mesh=torus, in_specs=placed, out_specs=P(AXES, None), check_vma=False)
```

```python
import jax
import jax.numpy as jnp
from jax import lax
from jax.experimental import pallas as pl
from jax.experimental.pallas import tpu as pltpu
from jax.sharding import Mesh
from jax.sharding import PartitionSpec as P

AXES = ("y", "x", "zl", "zh", "c")
SLABS = ("y", "x", "zl")
IPTS = ("zh", "c")
RING = 4
ORDER = (
    (0, 0), (0, 1), (0, 3), (1, 0), (3, 0), (1, 1), (3, 3), (1, 3), (3, 1), (0, 2), (2, 0),
    (1, 2), (3, 2), (2, 1), (2, 3), (2, 2),
)
NEAR, FAR, BASE, SIDE = 16, 18, 20, 21
NEXT = (((0, 1), "x", 1), ((0, 3), "x", -1), ((1, 0), "y", 1), ((3, 0), "y", -1))


def take_from(value, axis, side):
    n = lax.axis_size(axis)
    return lax.ppermute(value, axis, [((i + side) % n, i) for i in range(n)])


def after(value, *others):
    return lax.optimization_barrier((value, others))[0]


def pick_kernel(table, ids, orb, tgt, mine, theirs):
    rows, norb = orb.shape
    half = rows // 2
    bases = [table[BASE] + table[NEAR + k] * half for k in range(2)]
    for k, out in ((0, mine), (1, theirs)):
        row = lax.broadcasted_iota(jnp.int32, (rows, out.shape[0]), 0)
        row = row + jnp.where(row < half, bases[0], bases[1] - half)
        hot = (row == ids[k : k + 1, :]).astype(jnp.bfloat16)
        dims = (((0,), (0,)), ((), ()))
        out[:, :norb] = lax.dot_general(hot, orb[...], dims, preferred_element_type=jnp.float32).astype(out.dtype)
        out[:, norb:] = lax.dot_general(hot, tgt[...], dims, preferred_element_type=jnp.float32).astype(out.dtype)


def pick(table, ids, orb, tgt):
    out = jax.ShapeDtypeStruct((ids.shape[1], orb.shape[1] + tgt.shape[1]), orb.dtype)
    whole = pl.BlockSpec(memory_space=pltpu.VMEM)
    return pl.pallas_call(
        pick_kernel,
        out_shape=(out, out),
        in_specs=[pl.BlockSpec(memory_space=pltpu.SMEM)] + [whole] * 3,
        out_specs=(whole, whole),
        compiler_params=pltpu.CompilerParams(vmem_limit_bytes=32 << 20),
        name="pick",
    )(table, ids, orb, tgt)


def apply_parts(slab, parts, potential, table, row_at, col_at, count, total, last=False):
    tile = slab.shape[0] // 2
    norb = slab.shape[1]
    points = sum(p.shape[0] for p in parts) // count
    width = parts[0].shape[1]
    nj = width - norb
    first = total is None

    def body(t, slab_ref, *refs):
        ours, pots = refs[: len(parts)], refs[len(parts) : len(parts) + count]
        here = pl.ds(pl.multiple_of(pl.program_id(0) * tile, tile), tile)
        orb = jnp.concatenate([p[:, :norb] for p in ours], axis=0)
        tgt = jnp.concatenate([p[:, norb:] for p in ours], axis=0)
        products = lax.dot_general(
            slab_ref[here, :], orb, (((1,), (1,)), ((), ())), preferred_element_type=jnp.float32
        )
        pot = jnp.concatenate([p[...] for p in pots], axis=1)
        weighted = (pot.astype(jnp.float32) * products).astype(jnp.bfloat16)
        term = jnp.dot(weighted, tgt, preferred_element_type=jnp.float32)
        if not first:
            term = refs[len(parts) + count][here, :] + term
        if not last:
            refs[-1][here, :] = term
            return
        for k, out in enumerate(refs[-2:]):

            @pl.when(pl.program_id(0) == k)
            def _():
                out[...] = term

    def pot_spec(k):
        return pl.BlockSpec((tile, points), lambda i, t: (t[row_at + i], t[col_at + k]))

    whole = pl.BlockSpec(memory_space=pltpu.VMEM)
    specs = [whole] * (1 + len(parts)) + [pot_spec(k) for k in range(count)]
    args = [slab, *parts] + [potential] * count
    if not first:
        specs.append(whole)
        args.append(total)
    flops = slab.shape[0] * points * count * width // 2
    half = jax.ShapeDtypeStruct((tile, nj), jnp.float32)
    return pl.pallas_call(
        body,
        out_shape=(half, half) if last else jax.ShapeDtypeStruct((slab.shape[0], nj), jnp.float32),
        grid_spec=pltpu.PrefetchScalarGridSpec(
            num_scalar_prefetch=1, grid=(2,), in_specs=specs, out_specs=(whole,) * 2 if last else whole
        ),
        input_output_aliases={} if first or last else {len(args): 0},
        cost_estimate=pl.CostEstimate(
            flops=flops, bytes_accessed=count * slab.shape[0] * points * 2, transcendentals=0
        ),
        compiler_params=pltpu.CompilerParams(vmem_limit_bytes=15 << 20),
        name="apply",
    )(table, *args)


def local(orbitals, targets, points, potential):
    own_rows = orbitals.shape[0]
    potential = pltpu.with_memory_space_constraint(potential, pltpu.HBM)
    count = points.shape[1]
    y, x, zl, zh, c = (lax.axis_index(a) for a in AXES)
    slab_start = ((y * RING + x) * 2 + zl) * own_rows * 4

    n = lax.iota(jnp.int32, SIDE + 1)
    code = jnp.zeros_like(n)
    for k, (dy, dx) in enumerate(ORDER):
        code = jnp.where(n == k, dy * RING + dx, code)
    cols = (y + code // RING) % RING * RING + (x + code % RING) % RING
    half_at = jnp.where(n < FAR, zh, 1 - zh)
    rows = half_at * 2 + jnp.where((n - NEAR) % 2 == 0, c, 1 - c)
    table = jnp.where(n < NEAR, cols, jnp.where(n < BASE, rows, jnp.where(n < SIDE, slab_start, zl)))
    table = table.astype(jnp.int32)

    sib_orb = take_from(orbitals, "c", 1)
    sib_tgt = take_from(targets, "c", 1)
    far_points = take_from(points, "zh", 1)
    near_slab = jnp.concatenate([orbitals, sib_orb], axis=0)
    near_tgt = jnp.concatenate([targets, sib_tgt], axis=0)
    ids = jnp.concatenate([points, far_points], axis=0)
    mine, theirs = pick(table, ids, near_slab, near_tgt)
    block = mine + take_from(theirs, "zh", 1)
    lower = table[SIDE:].reshape(1, 1) == 0

    def in_order(own, other):
        return jnp.concatenate([jnp.where(lower, own, other), jnp.where(lower, other, own)], axis=0)

    def near_apply(parts, ats, total, last=False):
        return apply_parts(near_slab, parts, potential, table, NEAR, ORDER.index(ats[0]), len(ats), total, last)

    def far_apply(parts, ats, total, last=False):
        return apply_parts(far_slab, parts, potential, table, FAR, ORDER.index(ats[0]), len(ats), total, last)

    own = {at: take_from(block, axis, side) for at, axis, side in NEXT}
    other = take_from(block, "zl", 1)
    far_slab = take_from(after(near_slab, *own.values()), "zh", 1)
    pair = {at: in_order(own[at], take_from(other, axis, side)) for at, axis, side in NEXT}
    pair[0, 0] = in_order(block, other)

    def joined(whole, half):
        return jnp.concatenate([pair[whole], half], axis=0)

    from_right = take_from(joined((1, 0), pair[0, 1][:count]), "x", 1)
    from_left = take_from(joined((3, 0), pair[0, 3][count:]), "x", -1)
    from_up = take_from(joined((0, 3), pair[1, 0][:count]), "y", 1)
    from_down = take_from(joined((0, 1), pair[3, 0][count:]), "y", -1)
    first = ((0, 0), *(at for at, _, _ in NEXT))
    near = near_apply([pair[at] for at in first], first, None)
    from_right, from_left, from_up, from_down = lax.optimization_barrier(
        (from_right, from_left, from_up, from_down, near)
    )[:4]
    both = 2 * count
    pair[1, 1], pair[3, 3] = from_right[:both], from_left[:both]
    pair[1, 3], pair[3, 1] = from_up[:both], from_down[:both]
    pair[0, 2] = jnp.concatenate([from_right[both:], from_left[both:]], axis=0)
    pair[2, 0] = jnp.concatenate([from_up[both:], from_down[both:]], axis=0)

    pair[1, 2] = take_from(pair[1, 1], "x", 1)
    pair[3, 2] = take_from(pair[3, 3], "x", -1)
    pair[2, 1] = take_from(pair[1, 1], "y", 1)
    pair[2, 3] = take_from(pair[3, 3], "y", -1)
    second = ((1, 1), (3, 3), (1, 3), (3, 1), (0, 2), (2, 0))
    far = far_apply([pair[at] for at in first], first, None)
    far = far_apply([pair[at] for at in second], second, far)

    third = ((1, 2), (3, 2), (2, 1), (2, 3))
    ready = lax.optimization_barrier((*(pair[at] for at in third), far))[:4]
    pair.update(zip(third, ready))
    last = [take_from(pair[2, 1][:count], "x", 1), take_from(pair[1, 2][count:], "y", 1)]
    near = near_apply([pair[at] for at in second], second, after(near, far))
    third += ((2, 2),)
    last = [pair[at] for at in third[:4]] + last
    kept, sent = far_apply(last, third, after(far, near), True)
    far = (kept + take_from(sent, "c", 1)).astype(jnp.bfloat16)
    away = take_from(far, "zh", 1)
    kept, sent = near_apply(last, third, after(near, far), True)
    near = kept + take_from(after(sent, away), "c", 1)
    return (-(near + away.astype(jnp.float32))).astype(jnp.bfloat16)


def solution(mesh):
    torus = Mesh(mesh.devices.reshape(RING, RING, 2, 2, 2), AXES)
    placed = (P(AXES, None), P(AXES, None), P(IPTS, SLABS), P(SLABS, IPTS))
    return jax.shard_map(local, mesh=torus, in_specs=placed, out_specs=P(AXES, None), check_vma=False)
```

```python
import jax
import jax.numpy as jnp
from jax import lax
from jax.experimental import pallas as pl
from jax.experimental.pallas import tpu as pltpu
from jax.sharding import Mesh
from jax.sharding import PartitionSpec as P

AXES = ("y", "x", "zl", "zh", "c")
SLABS = ("y", "x", "zl")
IPTS = ("zh", "c")
RING = 4
ORDER = (
    (0, 0), (0, 1), (0, 3), (1, 0), (3, 0), (1, 1), (3, 3), (1, 3), (3, 1), (0, 2), (2, 0),
    (1, 2), (3, 2), (2, 1), (2, 3), (2, 2),
)
NEAR, FAR, BASE, SIDE = 16, 18, 20, 21
NEXT = (((0, 1), "x", 1), ((0, 3), "x", -1), ((1, 0), "y", 1), ((3, 0), "y", -1))


def take_from(value, axis, side):
    n = lax.axis_size(axis)
    return lax.ppermute(value, axis, [((i + side) % n, i) for i in range(n)])


def after(value, *others):
    return lax.optimization_barrier((value, others))[0]


def pick_kernel(table, ids, orb, own_tgt, sib_tgt, mine, theirs):
    rows, norb = orb.shape
    half = rows // 2
    bases = [table[BASE] + table[NEAR + k] * half for k in range(2)]
    for k, out in ((0, mine), (1, theirs)):
        row = lax.broadcasted_iota(jnp.int32, (rows, out.shape[0]), 0)
        row = row + jnp.where(row < half, bases[0], bases[1] - half)
        hot = (row == ids[k : k + 1, :]).astype(jnp.bfloat16)
        dims = (((0,), (0,)), ((), ()))
        out[:, :norb] = lax.dot_general(hot, orb[...], dims, preferred_element_type=jnp.float32).astype(out.dtype)
        picked = [
            lax.dot_general(hot[k * half : (k + 1) * half], tgt[...], dims, preferred_element_type=jnp.float32)
            for k, tgt in enumerate((own_tgt, sib_tgt))
        ]
        out[:, norb:] = (picked[0] + picked[1]).astype(out.dtype)


def pick(table, ids, orb, own_tgt, sib_tgt):
    out = jax.ShapeDtypeStruct((ids.shape[1], orb.shape[1] + own_tgt.shape[1]), orb.dtype)
    whole = pl.BlockSpec(memory_space=pltpu.VMEM)
    return pl.pallas_call(
        pick_kernel,
        out_shape=(out, out),
        in_specs=[pl.BlockSpec(memory_space=pltpu.SMEM)] + [whole] * 4,
        out_specs=(whole, whole),
        compiler_params=pltpu.CompilerParams(vmem_limit_bytes=32 << 20),
        name="pick",
    )(table, ids, orb, own_tgt, sib_tgt)


def apply_parts(slab, parts, potential, table, row_at, col_at, count, total, last=False):
    tile = slab.shape[0] // 2
    norb = slab.shape[1]
    points = sum(p.shape[0] for p in parts) // count
    width = parts[0].shape[1]
    nj = width - norb
    first = total is None

    def body(t, slab_ref, *refs):
        ours, pots = refs[: len(parts)], refs[len(parts) : len(parts) + count]
        here = pl.ds(pl.multiple_of(pl.program_id(0) * tile, tile), tile)
        orb = jnp.concatenate([p[:, :norb] for p in ours], axis=0)
        tgt = jnp.concatenate([p[:, norb:] for p in ours], axis=0)
        products = lax.dot_general(
            slab_ref[here, :], orb, (((1,), (1,)), ((), ())), preferred_element_type=jnp.float32
        )
        pot = jnp.concatenate([p[...] for p in pots], axis=1)
        weighted = (pot.astype(jnp.float32) * products).astype(jnp.bfloat16)
        term = jnp.dot(weighted, tgt, preferred_element_type=jnp.float32)
        if not first:
            term = refs[len(parts) + count][here, :] + term
        if not last:
            refs[-1][here, :] = term
            return
        for k, out in enumerate(refs[-2:]):

            @pl.when(pl.program_id(0) == k)
            def _():
                out[...] = term.astype(out.dtype)

    def pot_spec(k):
        return pl.BlockSpec((tile, points), lambda i, t: (t[row_at + i], t[col_at + k]))

    whole = pl.BlockSpec(memory_space=pltpu.VMEM)
    specs = [whole] * (1 + len(parts)) + [pot_spec(k) for k in range(count)]
    args = [slab, *parts] + [potential] * count
    if not first:
        specs.append(whole)
        args.append(total)
    flops = slab.shape[0] * points * count * width // 2
    halves = tuple(jax.ShapeDtypeStruct((tile, nj), t) for t in (jnp.float32, jnp.bfloat16))
    return pl.pallas_call(
        body,
        out_shape=halves if last else jax.ShapeDtypeStruct((slab.shape[0], nj), jnp.float32),
        grid_spec=pltpu.PrefetchScalarGridSpec(
            num_scalar_prefetch=1, grid=(2,), in_specs=specs, out_specs=(whole,) * 2 if last else whole
        ),
        input_output_aliases={} if first or last else {len(args): 0},
        cost_estimate=pl.CostEstimate(
            flops=flops, bytes_accessed=count * slab.shape[0] * points * 2, transcendentals=0
        ),
        compiler_params=pltpu.CompilerParams(vmem_limit_bytes=15 << 20),
        name="apply",
    )(table, *args)


def local(orbitals, targets, points, potential):
    own_rows = orbitals.shape[0]
    potential = pltpu.with_memory_space_constraint(potential, pltpu.HBM)
    count = points.shape[1]
    y, x, zl, zh, c = (lax.axis_index(a) for a in AXES)
    slab_start = ((y * RING + x) * 2 + zl) * own_rows * 4

    n = lax.iota(jnp.int32, SIDE + 1)
    code = jnp.zeros_like(n)
    for k, (dy, dx) in enumerate(ORDER):
        code = jnp.where(n == k, dy * RING + dx, code)
    cols = (y + code // RING) % RING * RING + (x + code % RING) % RING
    half_at = jnp.where(n < FAR, zh, 1 - zh)
    rows = half_at * 2 + jnp.where((n - NEAR) % 2 == 0, c, 1 - c)
    table = jnp.where(n < NEAR, cols, jnp.where(n < BASE, rows, jnp.where(n < SIDE, slab_start, zl)))
    table = table.astype(jnp.int32)

    sib_orb = take_from(orbitals, "c", 1)
    sib_tgt = take_from(targets, "c", 1)
    far_points = take_from(points, "zh", 1)
    near_slab = jnp.concatenate([orbitals, sib_orb], axis=0)
    ids = jnp.concatenate([points, far_points], axis=0)
    mine, theirs = pick(table, ids, near_slab, targets, sib_tgt)
    block = mine + take_from(theirs, "zh", 1)
    lower = table[SIDE:].reshape(1, 1) == 0

    def in_order(own, other):
        return jnp.concatenate([jnp.where(lower, own, other), jnp.where(lower, other, own)], axis=0)

    def near_apply(parts, ats, total, last=False):
        return apply_parts(near_slab, parts, potential, table, NEAR, ORDER.index(ats[0]), len(ats), total, last)

    def far_apply(parts, ats, total, last=False):
        return apply_parts(far_slab, parts, potential, table, FAR, ORDER.index(ats[0]), len(ats), total, last)

    own = {at: take_from(block, axis, side) for at, axis, side in NEXT}
    other = take_from(block, "zl", 1)
    far_slab = take_from(after(near_slab, *own.values()), "zh", 1)
    pair = {at: in_order(own[at], take_from(other, axis, side)) for at, axis, side in NEXT}
    pair[0, 0] = in_order(block, other)

    def joined(whole, half):
        return jnp.concatenate([pair[whole], half], axis=0)

    from_right = take_from(joined((1, 0), pair[0, 1][:count]), "x", 1)
    from_left = take_from(joined((3, 0), pair[0, 3][count:]), "x", -1)
    from_up = take_from(joined((0, 3), pair[1, 0][:count]), "y", 1)
    from_down = take_from(joined((0, 1), pair[3, 0][count:]), "y", -1)
    first = ((0, 0), *(at for at, _, _ in NEXT))
    near = near_apply([pair[at] for at in first], first, None)
    from_right, from_left = after(from_right, near), after(from_left, near)
    both = 2 * count
    pair[1, 1], pair[3, 3] = from_right[:both], from_left[:both]
    pair[1, 3], pair[3, 1] = from_up[:both], from_down[:both]
    pair[0, 2] = jnp.concatenate([from_right[both:], from_left[both:]], axis=0)
    pair[2, 0] = jnp.concatenate([from_up[both:], from_down[both:]], axis=0)

    pair[1, 2] = take_from(pair[1, 1], "x", 1)
    pair[3, 2] = take_from(pair[3, 3], "x", -1)
    pair[2, 1] = take_from(pair[1, 1], "y", 1)
    pair[2, 3] = take_from(pair[3, 3], "y", -1)
    second = ((1, 1), (3, 3), (1, 3), (3, 1), (0, 2), (2, 0))
    far = far_apply([pair[at] for at in first], first, None)
    far = far_apply([pair[at] for at in second], second, far)

    third = ((1, 2), (3, 2), (2, 1), (2, 3))
    pair[2, 1], pair[1, 2] = after(pair[2, 1], far), after(pair[1, 2], far)
    last = [take_from(pair[2, 1][:count], "x", 1), take_from(pair[1, 2][count:], "y", 1)]
    near = near_apply([pair[at] for at in second], second, after(near, far))
    third += ((2, 2),)
    last = [pair[at] for at in third[:4]] + last
    kept, sent = far_apply(last, third, after(far, near), True)
    far = (kept + take_from(sent, "c", 1)).astype(jnp.bfloat16)
    away = take_from(far, "zh", 1)
    kept, sent = near_apply(last, third, after(near, far), True)
    near = kept + take_from(after(sent, away), "c", 1)
    return (-(near + away.astype(jnp.float32))).astype(jnp.bfloat16)


def solution(mesh):
    torus = Mesh(mesh.devices.reshape(RING, RING, 2, 2, 2), AXES)
    placed = (P(AXES, None), P(AXES, None), P(IPTS, SLABS), P(SLABS, IPTS))
    return jax.shard_map(local, mesh=torus, in_specs=placed, out_specs=P(AXES, None), check_vma=False)
```

```python
import jax
import jax.numpy as jnp
from jax import lax
from jax.experimental import pallas as pl
from jax.experimental.pallas import tpu as pltpu
from jax.sharding import Mesh
from jax.sharding import PartitionSpec as P

AXES = ("y", "x", "zl", "zh", "c")
SLABS = ("y", "x", "zl")
IPTS = ("zh", "c")
RING = 4
ORDER = (
    (0, 0), (0, 1), (0, 3), (1, 0), (3, 0), (1, 1), (3, 3), (1, 3), (3, 1), (0, 2), (2, 0),
    (2, 1), (2, 3), (3, 2), (1, 2), (2, 2),
)
NEAR, FAR, BASE, SIDE = 16, 18, 20, 21
NEXT = (((0, 1), "x", 1), ((0, 3), "x", -1), ((1, 0), "y", 1), ((3, 0), "y", -1))


def take_from(value, axis, side):
    n = lax.axis_size(axis)
    return lax.ppermute(value, axis, [((i + side) % n, i) for i in range(n)])


def after(value, *others):
    return lax.optimization_barrier((value, others))[0]


def pick_kernel(table, ids, orb, own_tgt, sib_tgt, mine, theirs):
    rows, norb = orb.shape
    half = rows // 2
    bases = [table[BASE] + table[NEAR + k] * half for k in range(2)]
    for k, out in ((0, mine), (1, theirs)):
        row = lax.broadcasted_iota(jnp.int32, (rows, out.shape[0]), 0)
        row = row + jnp.where(row < half, bases[0], bases[1] - half)
        hot = (row == ids[k : k + 1, :]).astype(jnp.bfloat16)
        dims = (((0,), (0,)), ((), ()))
        out[:, :norb] = lax.dot_general(hot, orb[...], dims, preferred_element_type=jnp.float32).astype(out.dtype)
        picked = [
            lax.dot_general(hot[k * half : (k + 1) * half], tgt[...], dims, preferred_element_type=jnp.float32)
            for k, tgt in enumerate((own_tgt, sib_tgt))
        ]
        out[:, norb:] = (picked[0] + picked[1]).astype(out.dtype)


def pick(table, ids, orb, own_tgt, sib_tgt):
    out = jax.ShapeDtypeStruct((ids.shape[1], orb.shape[1] + own_tgt.shape[1]), orb.dtype)
    whole = pl.BlockSpec(memory_space=pltpu.VMEM)
    return pl.pallas_call(
        pick_kernel,
        out_shape=(out, out),
        in_specs=[pl.BlockSpec(memory_space=pltpu.SMEM)] + [whole] * 4,
        out_specs=(whole, whole),
        compiler_params=pltpu.CompilerParams(vmem_limit_bytes=32 << 20),
        name="pick",
    )(table, ids, orb, own_tgt, sib_tgt)


def apply_parts(slab, parts, potential, table, row_at, col_at, count, total, last=False):
    tile = slab.shape[0] // 2
    norb = slab.shape[1]
    points = sum(p.shape[0] for p in parts) // count
    width = parts[0].shape[1]
    nj = width - norb
    first = total is None

    def body(t, slab_ref, *refs):
        ours, pots = refs[: len(parts)], refs[len(parts) : len(parts) + count]
        here = pl.ds(pl.multiple_of(pl.program_id(0) * tile, tile), tile)
        orb = jnp.concatenate([p[:, :norb] for p in ours], axis=0)
        tgt = jnp.concatenate([p[:, norb:] for p in ours], axis=0)
        products = lax.dot_general(
            slab_ref[here, :], orb, (((1,), (1,)), ((), ())), preferred_element_type=jnp.float32
        )
        pot = jnp.concatenate([p[...] for p in pots], axis=1)
        weighted = (pot.astype(jnp.float32) * products).astype(jnp.bfloat16)
        term = jnp.dot(weighted, tgt, preferred_element_type=jnp.float32)
        if not first:
            term = refs[len(parts) + count][here, :] + term
        if not last:
            refs[-1][here, :] = term
            return
        for k, out in enumerate(refs[-2:]):

            @pl.when(pl.program_id(0) == k)
            def _():
                out[...] = term.astype(out.dtype)

    def pot_spec(k):
        return pl.BlockSpec((tile, points), lambda i, t: (t[row_at + i], t[col_at + k]))

    whole = pl.BlockSpec(memory_space=pltpu.VMEM)
    specs = [whole] * (1 + len(parts)) + [pot_spec(k) for k in range(count)]
    args = [slab, *parts] + [potential] * count
    if not first:
        specs.append(whole)
        args.append(total)
    flops = slab.shape[0] * points * count * width // 2
    halves = tuple(jax.ShapeDtypeStruct((tile, nj), t) for t in (jnp.float32, jnp.bfloat16))
    return pl.pallas_call(
        body,
        out_shape=halves if last else jax.ShapeDtypeStruct((slab.shape[0], nj), jnp.float32),
        grid_spec=pltpu.PrefetchScalarGridSpec(
            num_scalar_prefetch=1, grid=(2,), in_specs=specs, out_specs=(whole,) * 2 if last else whole
        ),
        input_output_aliases={} if first or last else {len(args): 0},
        cost_estimate=pl.CostEstimate(
            flops=flops, bytes_accessed=count * slab.shape[0] * points * 2, transcendentals=0
        ),
        compiler_params=pltpu.CompilerParams(vmem_limit_bytes=15 << 20),
        name="apply",
    )(table, *args)


def local(orbitals, targets, points, potential):
    own_rows = orbitals.shape[0]
    potential = pltpu.with_memory_space_constraint(potential, pltpu.HBM)
    count = points.shape[1]
    y, x, zl, zh, c = (lax.axis_index(a) for a in AXES)
    slab_start = ((y * RING + x) * 2 + zl) * own_rows * 4

    n = lax.iota(jnp.int32, SIDE + 1)
    code = jnp.zeros_like(n)
    for k, (dy, dx) in enumerate(ORDER):
        code = jnp.where(n == k, dy * RING + dx, code)
    cols = (y + code // RING) % RING * RING + (x + code % RING) % RING
    half_at = jnp.where(n < FAR, zh, 1 - zh)
    rows = half_at * 2 + jnp.where((n - NEAR) % 2 == 0, c, 1 - c)
    table = jnp.where(n < NEAR, cols, jnp.where(n < BASE, rows, jnp.where(n < SIDE, slab_start, zl)))
    table = table.astype(jnp.int32)

    sib_orb = take_from(orbitals, "c", 1)
    sib_tgt = take_from(targets, "c", 1)
    far_points = take_from(points, "zh", 1)
    near_slab = jnp.concatenate([orbitals, sib_orb], axis=0)
    ids = jnp.concatenate([points, far_points], axis=0)
    mine, theirs = pick(table, ids, near_slab, targets, sib_tgt)
    block = mine + take_from(theirs, "zh", 1)
    lower = table[SIDE:].reshape(1, 1) == 0

    def in_order(own, other):
        return jnp.concatenate([jnp.where(lower, own, other), jnp.where(lower, other, own)], axis=0)

    def near_apply(parts, ats, total, last=False):
        return apply_parts(near_slab, parts, potential, table, NEAR, ORDER.index(ats[0]), len(ats), total, last)

    def far_apply(parts, ats, total, last=False):
        return apply_parts(far_slab, parts, potential, table, FAR, ORDER.index(ats[0]), len(ats), total, last)

    own = {at: take_from(block, axis, side) for at, axis, side in NEXT}
    other = take_from(block, "zl", 1)
    far_slab = take_from(after(near_slab, *own.values()), "zh", 1)
    pair = {at: in_order(own[at], take_from(other, axis, side)) for at, axis, side in NEXT}
    pair[0, 0] = in_order(block, other)

    def joined(whole, half):
        return jnp.concatenate([pair[whole], half], axis=0)

    from_right = take_from(joined((1, 0), pair[0, 1][:count]), "x", 1)
    from_left = take_from(joined((3, 0), pair[0, 3][count:]), "x", -1)
    from_up = take_from(joined((0, 3), pair[1, 0][:count]), "y", 1)
    from_down = take_from(joined((0, 1), pair[3, 0][count:]), "y", -1)
    first = ((0, 0), *(at for at, _, _ in NEXT))
    near = near_apply([pair[at] for at in first], first, None)
    both = 2 * count
    from_right, from_left, from_up, from_down = (after(v, near) for v in (from_right, from_left, from_up, from_down))
    pair[1, 1], pair[3, 3] = from_right[:both], from_left[:both]
    pair[1, 3], pair[3, 1] = from_up[:both], from_down[:both]
    pair[0, 2] = jnp.concatenate([from_right[both:], from_left[both:]], axis=0)
    pair[2, 0] = jnp.concatenate([from_up[both:], from_down[both:]], axis=0)

    second = ((1, 1), (3, 3), (1, 3), (3, 1), (0, 2), (2, 0))
    third = ((2, 1), (2, 3), (3, 2), (1, 2), (2, 2))
    last = [
        take_from(jnp.concatenate([pair[1, 1], pair[1, 3][:count]], axis=0), "y", 1),
        take_from(jnp.concatenate([pair[3, 3][count:], pair[0, 2]], axis=0), "y", -1),
        take_from(pair[1, 1][:count], "x", 1),
        take_from(pair[1, 3][count:], "x", -1),
        take_from(pair[2, 0], "x", 2),
    ]
    far = far_apply([pair[at] for at in first], first, None)
    far = far_apply([pair[at] for at in second], second, far)
    near = near_apply([pair[at] for at in second], second, after(near, far))
    last, far, near = lax.optimization_barrier((last, far, near))
    kept, sent = far_apply(last, third, far, True)
    far = (kept + take_from(sent, "c", 1)).astype(jnp.bfloat16)
    away = take_from(far, "zh", 1)
    kept, sent = near_apply(last, third, after(near, far), True)
    near = kept + take_from(after(sent, away), "c", 1)
    return (-(near + away.astype(jnp.float32))).astype(jnp.bfloat16)


def solution(mesh):
    torus = Mesh(mesh.devices.reshape(RING, RING, 2, 2, 2), AXES)
    placed = (P(AXES, None), P(AXES, None), P(IPTS, SLABS), P(SLABS, IPTS))
    return jax.shard_map(local, mesh=torus, in_specs=placed, out_specs=P(AXES, None), check_vma=False)
```

```python
import jax
import jax.numpy as jnp
from jax import lax
from jax.experimental import pallas as pl
from jax.experimental.pallas import tpu as pltpu
from jax.sharding import Mesh
from jax.sharding import PartitionSpec as P

AXES = ("y", "x", "zl", "zh", "c")
SLABS = ("y", "x", "zl")
IPTS = ("zh", "c")
RING = 4
ORDER = (
    (0, 0), (0, 1), (0, 3), (1, 0), (3, 0), (1, 1), (3, 3), (1, 3), (3, 1), (0, 2), (2, 0),
    (2, 1), (2, 3), (3, 2), (1, 2), (2, 2),
)
NEAR, FAR, BASE, SIDE = 16, 18, 20, 21
NEXT = (((0, 1), "x", 1), ((0, 3), "x", -1), ((1, 0), "y", 1), ((3, 0), "y", -1))


def take_from(value, axis, side):
    n = lax.axis_size(axis)
    return lax.ppermute(value, axis, [((i + side) % n, i) for i in range(n)])


def after(value, *others):
    return lax.optimization_barrier((value, others))[0]


def pick_kernel(table, ids, orb, own_tgt, sib_tgt, mine, theirs):
    rows, norb = orb.shape
    half = rows // 2
    bases = [table[BASE] + table[NEAR + k] * half for k in range(2)]
    for k, out in ((0, mine), (1, theirs)):
        row = lax.broadcasted_iota(jnp.int32, (rows, out.shape[0]), 0)
        row = row + jnp.where(row < half, bases[0], bases[1] - half)
        hot = (row == ids[k : k + 1, :]).astype(jnp.bfloat16)
        dims = (((0,), (0,)), ((), ()))
        out[:, :norb] = lax.dot_general(hot, orb[...], dims, preferred_element_type=jnp.float32).astype(out.dtype)
        picked = [
            lax.dot_general(hot[k * half : (k + 1) * half], tgt[...], dims, preferred_element_type=jnp.float32)
            for k, tgt in enumerate((own_tgt, sib_tgt))
        ]
        out[:, norb:] = (picked[0] + picked[1]).astype(out.dtype)


def pick(table, ids, orb, own_tgt, sib_tgt):
    out = jax.ShapeDtypeStruct((ids.shape[1], orb.shape[1] + own_tgt.shape[1]), orb.dtype)
    whole = pl.BlockSpec(memory_space=pltpu.VMEM)
    return pl.pallas_call(
        pick_kernel,
        out_shape=(out, out),
        in_specs=[pl.BlockSpec(memory_space=pltpu.SMEM)] + [whole] * 4,
        out_specs=(whole, whole),
        compiler_params=pltpu.CompilerParams(vmem_limit_bytes=32 << 20),
        name="pick",
    )(table, ids, orb, own_tgt, sib_tgt)


def apply_parts(slab, parts, potential, table, row_at, col_at, count, total, last=False):
    tile = slab.shape[0] // 2
    norb = slab.shape[1]
    points = sum(p.shape[0] for p in parts) // count
    width = parts[0].shape[1]
    nj = width - norb
    first = total is None

    def body(t, slab_ref, *refs):
        ours, pots = refs[: len(parts)], refs[len(parts) : len(parts) + count]
        here = pl.ds(pl.multiple_of(pl.program_id(0) * tile, tile), tile)
        orb = jnp.concatenate([p[:, :norb] for p in ours], axis=0)
        tgt = jnp.concatenate([p[:, norb:] for p in ours], axis=0)
        products = lax.dot_general(
            slab_ref[here, :], orb, (((1,), (1,)), ((), ())), preferred_element_type=jnp.float32
        )
        pot = jnp.concatenate([p[...] for p in pots], axis=1)
        weighted = (pot.astype(jnp.float32) * products).astype(jnp.bfloat16)
        term = jnp.dot(weighted, tgt, preferred_element_type=jnp.float32)
        if not first:
            term = refs[len(parts) + count][here, :] + term
        if not last:
            refs[-1][here, :] = term
            return
        for k, out in enumerate(refs[-2:]):

            @pl.when(pl.program_id(0) == k)
            def _():
                out[...] = term.astype(out.dtype)

    def pot_spec(k):
        return pl.BlockSpec((tile, points), lambda i, t: (t[row_at + i], t[col_at + k]))

    whole = pl.BlockSpec(memory_space=pltpu.VMEM)
    specs = [whole] * (1 + len(parts)) + [pot_spec(k) for k in range(count)]
    args = [slab, *parts] + [potential] * count
    if not first:
        specs.append(whole)
        args.append(total)
    flops = slab.shape[0] * points * count * width // 2
    halves = tuple(jax.ShapeDtypeStruct((tile, nj), t) for t in (jnp.float32, jnp.bfloat16))
    return pl.pallas_call(
        body,
        out_shape=halves if last else jax.ShapeDtypeStruct((slab.shape[0], nj), jnp.float32),
        grid_spec=pltpu.PrefetchScalarGridSpec(
            num_scalar_prefetch=1, grid=(2,), in_specs=specs, out_specs=(whole,) * 2 if last else whole
        ),
        input_output_aliases={} if first or last else {len(args): 0},
        cost_estimate=pl.CostEstimate(
            flops=flops, bytes_accessed=count * slab.shape[0] * points * 2, transcendentals=0
        ),
        compiler_params=pltpu.CompilerParams(vmem_limit_bytes=15 << 20),
        name="apply",
    )(table, *args)


def local(orbitals, targets, points, potential):
    own_rows = orbitals.shape[0]
    potential = pltpu.with_memory_space_constraint(potential, pltpu.HBM)
    count = points.shape[1]
    y, x, zl, zh, c = (lax.axis_index(a) for a in AXES)
    slab_start = ((y * RING + x) * 2 + zl) * own_rows * 4

    n = lax.iota(jnp.int32, SIDE + 1)
    code = jnp.zeros_like(n)
    for k, (dy, dx) in enumerate(ORDER):
        code = jnp.where(n == k, dy * RING + dx, code)
    cols = (y + code // RING) % RING * RING + (x + code % RING) % RING
    half_at = jnp.where(n < FAR, zh, 1 - zh)
    rows = half_at * 2 + jnp.where((n - NEAR) % 2 == 0, c, 1 - c)
    table = jnp.where(n < NEAR, cols, jnp.where(n < BASE, rows, jnp.where(n < SIDE, slab_start, zl)))
    table = table.astype(jnp.int32)

    sib_orb = take_from(orbitals, "c", 1)
    sib_tgt = take_from(targets, "c", 1)
    far_points = take_from(points, "zh", 1)
    near_slab = jnp.concatenate([orbitals, sib_orb], axis=0)
    ids = jnp.concatenate([points, far_points], axis=0)
    mine, theirs = pick(table, ids, near_slab, targets, sib_tgt)
    block = mine + take_from(theirs, "zh", 1)
    lower = table[SIDE:].reshape(1, 1) == 0

    def in_order(own, other):
        return jnp.concatenate([jnp.where(lower, own, other), jnp.where(lower, other, own)], axis=0)

    def near_apply(parts, ats, total, last=False):
        return apply_parts(near_slab, parts, potential, table, NEAR, ORDER.index(ats[0]), len(ats), total, last)

    def far_apply(parts, ats, total, last=False):
        return apply_parts(far_slab, parts, potential, table, FAR, ORDER.index(ats[0]), len(ats), total, last)

    own = {at: take_from(block, axis, side) for at, axis, side in NEXT}
    other = take_from(block, "zl", 1)
    far_slab = take_from(after(near_slab, *own.values()), "zh", 1)
    pair = {(0, 0): in_order(block, other)}
    other = after(other, *own.values())
    for at, axis, side in NEXT:
        pair[at] = in_order(own[at], take_from(other, axis, side))

    def joined(whole, half):
        return jnp.concatenate([pair[whole], half], axis=0)

    from_right = take_from(joined((1, 0), pair[0, 1][:count]), "x", 1)
    from_left = take_from(joined((3, 0), pair[0, 3][count:]), "x", -1)
    from_up = take_from(joined((0, 3), pair[1, 0][:count]), "y", 1)
    from_down = take_from(joined((0, 1), pair[3, 0][count:]), "y", -1)
    first = ((0, 0), *(at for at, _, _ in NEXT))
    near = near_apply([pair[at] for at in first], first, None)
    both = 2 * count
    from_right, from_left, from_up, from_down = (after(v, near) for v in (from_right, from_left, from_up, from_down))
    pair[1, 1], pair[3, 3] = from_right[:both], from_left[:both]
    pair[1, 3], pair[3, 1] = from_up[:both], from_down[:both]
    pair[0, 2] = jnp.concatenate([from_right[both:], from_left[both:]], axis=0)
    pair[2, 0] = jnp.concatenate([from_up[both:], from_down[both:]], axis=0)

    second = ((1, 1), (3, 3), (1, 3), (3, 1), (0, 2), (2, 0))
    third = ((2, 1), (2, 3), (3, 2), (1, 2), (2, 2))
    last = [
        take_from(jnp.concatenate([pair[1, 1], pair[1, 3][:count]], axis=0), "y", 1),
        take_from(jnp.concatenate([pair[3, 3][count:], pair[0, 2]], axis=0), "y", -1),
        take_from(pair[1, 1][:count], "x", 1),
        take_from(pair[1, 3][count:], "x", -1),
        take_from(pair[2, 0], "x", 2),
    ]
    far = far_apply([pair[at] for at in first + second], first + second, None)
    near = near_apply([pair[at] for at in second], second, after(near, far))
    last, far, near = lax.optimization_barrier((last, far, near))
    kept, sent = far_apply(last, third, far, True)
    far = (kept + take_from(sent, "c", 1)).astype(jnp.bfloat16)
    away = take_from(far, "zh", 1)
    kept, sent = near_apply(last, third, after(near, far), True)
    near = kept + take_from(after(sent, away), "c", 1)
    return (-(near + away.astype(jnp.float32))).astype(jnp.bfloat16)


def solution(mesh):
    torus = Mesh(mesh.devices.reshape(RING, RING, 2, 2, 2), AXES)
    placed = (P(AXES, None), P(AXES, None), P(IPTS, SLABS), P(SLABS, IPTS))
    return jax.shard_map(local, mesh=torus, in_specs=placed, out_specs=P(AXES, None), check_vma=False)
```

```python
import jax
import jax.numpy as jnp
from jax import lax
from jax.experimental import pallas as pl
from jax.experimental.pallas import tpu as pltpu
from jax.sharding import Mesh
from jax.sharding import PartitionSpec as P

AXES = ("y", "x", "zl", "zh", "c")
SLABS = ("y", "x", "zl")
IPTS = ("zh", "c")
RING = 4
ORDER = (
    (0, 0), (0, 1), (0, 3), (1, 0), (3, 0), (1, 1), (3, 3), (1, 3), (3, 1), (0, 2), (2, 0),
    (2, 1), (2, 3), (3, 2), (1, 2), (2, 2),
)
NEAR, FAR, BASE, SIDE = 16, 18, 20, 21
NEXT = (((0, 1), "x", 1), ((0, 3), "x", -1), ((1, 0), "y", 1), ((3, 0), "y", -1))


def take_from(value, axis, side):
    n = lax.axis_size(axis)
    return lax.ppermute(value, axis, [((i + side) % n, i) for i in range(n)])


def after(value, *others):
    return lax.optimization_barrier((value, others))[0]


def pick_kernel(table, ids, orb, own_tgt, sib_tgt, mine, theirs):
    rows, norb = orb.shape
    half = rows // 2
    bases = [table[BASE] + table[NEAR + k] * half for k in range(2)]
    for k, out in ((0, mine), (1, theirs)):
        row = lax.broadcasted_iota(jnp.int32, (rows, out.shape[0]), 0)
        row = row + jnp.where(row < half, bases[0], bases[1] - half)
        hot = (row == ids[k : k + 1, :]).astype(jnp.bfloat16)
        dims = (((0,), (0,)), ((), ()))
        out[:, :norb] = lax.dot_general(hot, orb[...], dims, preferred_element_type=jnp.float32).astype(out.dtype)
        picked = [
            lax.dot_general(hot[k * half : (k + 1) * half], tgt[...], dims, preferred_element_type=jnp.float32)
            for k, tgt in enumerate((own_tgt, sib_tgt))
        ]
        out[:, norb:] = (picked[0] + picked[1]).astype(out.dtype)


def pick(table, ids, orb, own_tgt, sib_tgt):
    out = jax.ShapeDtypeStruct((ids.shape[1], orb.shape[1] + own_tgt.shape[1]), orb.dtype)
    whole = pl.BlockSpec(memory_space=pltpu.VMEM)
    return pl.pallas_call(
        pick_kernel,
        out_shape=(out, out),
        in_specs=[pl.BlockSpec(memory_space=pltpu.SMEM)] + [whole] * 4,
        out_specs=(whole, whole),
        compiler_params=pltpu.CompilerParams(vmem_limit_bytes=32 << 20),
        name="pick",
    )(table, ids, orb, own_tgt, sib_tgt)


def apply_parts(slab, parts, potential, table, row_at, col_at, count, total, last=False):
    tile = slab.shape[0] // 2
    norb = slab.shape[1]
    points = sum(p.shape[0] for p in parts) // count
    width = parts[0].shape[1]
    nj = width - norb
    first = total is None

    def body(t, slab_ref, *refs):
        ours, pots = refs[: len(parts)], refs[len(parts) : len(parts) + count]
        here = pl.ds(pl.multiple_of(pl.program_id(0) * tile, tile), tile)
        orb = jnp.concatenate([p[:, :norb] for p in ours], axis=0)
        tgt = jnp.concatenate([p[:, norb:] for p in ours], axis=0)
        products = lax.dot_general(
            slab_ref[here, :], orb, (((1,), (1,)), ((), ())), preferred_element_type=jnp.float32
        )
        pot = jnp.concatenate([p[...] for p in pots], axis=1)
        weighted = (pot.astype(jnp.float32) * products).astype(jnp.bfloat16)
        term = jnp.dot(weighted, tgt, preferred_element_type=jnp.float32)
        if not first:
            term = refs[len(parts) + count][here, :] + term
        if not last:
            refs[-1][here, :] = term
            return
        for k, out in enumerate(refs[-2:]):

            @pl.when(pl.program_id(0) == k)
            def _():
                out[...] = term.astype(out.dtype)

    def pot_spec(k):
        return pl.BlockSpec((tile, points), lambda i, t: (t[row_at + i], t[col_at + k]))

    whole = pl.BlockSpec(memory_space=pltpu.VMEM)
    specs = [whole] * (1 + len(parts)) + [pot_spec(k) for k in range(count)]
    args = [slab, *parts] + [potential] * count
    if not first:
        specs.append(whole)
        args.append(total)
    flops = slab.shape[0] * points * count * width // 2
    halves = tuple(jax.ShapeDtypeStruct((tile, nj), t) for t in (jnp.float32, jnp.bfloat16))
    return pl.pallas_call(
        body,
        out_shape=halves if last else jax.ShapeDtypeStruct((slab.shape[0], nj), jnp.float32),
        grid_spec=pltpu.PrefetchScalarGridSpec(
            num_scalar_prefetch=1, grid=(2,), in_specs=specs, out_specs=(whole,) * 2 if last else whole
        ),
        input_output_aliases={} if first or last else {len(args): 0},
        cost_estimate=pl.CostEstimate(
            flops=flops, bytes_accessed=count * slab.shape[0] * points * 2, transcendentals=0
        ),
        compiler_params=pltpu.CompilerParams(vmem_limit_bytes=15 << 20),
        name="apply",
    )(table, *args)


def local(orbitals, targets, points, potential):
    own_rows = orbitals.shape[0]
    potential = pltpu.with_memory_space_constraint(potential, pltpu.HBM)
    count = points.shape[1]
    y, x, zl, zh, c = (lax.axis_index(a) for a in AXES)
    slab_start = ((y * RING + x) * 2 + zl) * own_rows * 4

    n = lax.iota(jnp.int32, SIDE + 1)
    code = jnp.zeros_like(n)
    for k, (dy, dx) in enumerate(ORDER):
        code = jnp.where(n == k, dy * RING + dx, code)
    cols = (y + code // RING) % RING * RING + (x + code % RING) % RING
    half_at = jnp.where(n < FAR, zh, 1 - zh)
    rows = half_at * 2 + jnp.where((n - NEAR) % 2 == 0, c, 1 - c)
    table = jnp.where(n < NEAR, cols, jnp.where(n < BASE, rows, jnp.where(n < SIDE, slab_start, zl)))
    table = table.astype(jnp.int32)

    sib_orb = take_from(orbitals, "c", 1)
    sib_tgt = take_from(targets, "c", 1)
    far_points = take_from(points, "zh", 1)
    near_slab = jnp.concatenate([orbitals, sib_orb], axis=0)
    ids = jnp.concatenate([points, far_points], axis=0)
    mine, theirs = pick(table, ids, near_slab, targets, sib_tgt)
    block = mine + take_from(theirs, "zh", 1)
    lower = table[SIDE:].reshape(1, 1) == 0

    def in_order(own, other):
        return jnp.concatenate([jnp.where(lower, own, other), jnp.where(lower, other, own)], axis=0)

    def near_apply(parts, ats, total, last=False):
        return apply_parts(near_slab, parts, potential, table, NEAR, ORDER.index(ats[0]), len(ats), total, last)

    def far_apply(parts, ats, total, last=False):
        return apply_parts(far_slab, parts, potential, table, FAR, ORDER.index(ats[0]), len(ats), total, last)

    own = {at: take_from(block, axis, side) for at, axis, side in NEXT}
    other = take_from(block, "zl", 1)
    far_slab = take_from(after(near_slab, *own.values()), "zh", 1)
    pair = {(0, 0): in_order(block, other)}
    other = after(other, *own.values())
    for at, axis, side in NEXT:
        pair[at] = in_order(own[at], take_from(other, axis, side))

    def joined(whole, half):
        return jnp.concatenate([pair[whole], half], axis=0)

    from_right = take_from(joined((1, 0), pair[0, 1][:count]), "x", 1)
    from_left = take_from(joined((3, 0), pair[0, 3][count:]), "x", -1)
    from_up = take_from(joined((0, 3), pair[1, 0][:count]), "y", 1)
    from_down = take_from(joined((0, 1), pair[3, 0][count:]), "y", -1)
    first = ((0, 0), *(at for at, _, _ in NEXT))
    near = near_apply([pair[at] for at in first], first, None)
    both = 2 * count
    from_right, from_left, from_up, from_down = (after(v, near) for v in (from_right, from_left, from_up, from_down))
    pair[1, 1], pair[3, 3] = from_right[:both], from_left[:both]
    pair[1, 3], pair[3, 1] = from_up[:both], from_down[:both]
    pair[0, 2] = jnp.concatenate([from_right[both:], from_left[both:]], axis=0)
    pair[2, 0] = jnp.concatenate([from_up[both:], from_down[both:]], axis=0)

    second = ((1, 1), (3, 3), (1, 3), (3, 1), (0, 2), (2, 0))
    third = ((2, 1), (2, 3), (3, 2), (1, 2), (2, 2))
    last = [
        take_from(jnp.concatenate([pair[1, 1], pair[1, 3][:count]], axis=0), "y", 1),
        take_from(jnp.concatenate([pair[3, 3][count:], pair[0, 2]], axis=0), "y", -1),
        take_from(pair[1, 1][:count], "x", 1),
        pair[1, 3][count:],
        take_from(pair[2, 0], "x", 2),
    ]
    near = near_apply([pair[at] for at in second], second, near)
    last[3] = take_from(after(last[3], near), "x", -1)
    far_slab = after(far_slab, near)
    far = far_apply([pair[at] for at in first + second], first + second, None)
    last, far, near = lax.optimization_barrier((last, far, near))
    kept, sent = far_apply(last, third, far, True)
    far = (kept + take_from(sent, "c", 1)).astype(jnp.bfloat16)
    away = take_from(far, "zh", 1)
    kept, sent = near_apply(last, third, after(near, far), True)
    near = kept + take_from(after(sent, away), "c", 1)
    return (-(near + away.astype(jnp.float32))).astype(jnp.bfloat16)


def solution(mesh):
    torus = Mesh(mesh.devices.reshape(RING, RING, 2, 2, 2), AXES)
    placed = (P(AXES, None), P(AXES, None), P(IPTS, SLABS), P(SLABS, IPTS))
    return jax.shard_map(local, mesh=torus, in_specs=placed, out_specs=P(AXES, None), check_vma=False)
```

```python
import jax
import jax.numpy as jnp
from jax import lax
from jax.experimental import pallas as pl
from jax.experimental.pallas import tpu as pltpu
from jax.sharding import Mesh
from jax.sharding import PartitionSpec as P

AXES = ("y", "x", "zl", "zh", "c")
SLABS = ("y", "x", "zl")
IPTS = ("zh", "c")
RING = 4
ORDER = (
    (0, 0), (0, 1), (0, 3), (1, 0), (3, 0), (1, 1), (3, 3), (1, 3), (3, 1), (0, 2), (2, 0),
    (2, 1), (2, 3), (3, 2), (1, 2), (2, 2),
)
NEAR, FAR, BASE, SIDE = 16, 18, 20, 21
NEXT = (((0, 1), "x", 1), ((0, 3), "x", -1), ((1, 0), "y", 1), ((3, 0), "y", -1))


def take_from(value, axis, side):
    n = lax.axis_size(axis)
    return lax.ppermute(value, axis, [((i + side) % n, i) for i in range(n)])


def after(value, *others):
    return lax.optimization_barrier((value, others))[0]


def pick_kernel(table, ids, orb, own_tgt, sib_tgt, mine, theirs):
    rows, norb = orb.shape
    half = rows // 2
    bases = [table[BASE] + table[NEAR + k] * half for k in range(2)]
    for k, out in ((0, mine), (1, theirs)):
        row = lax.broadcasted_iota(jnp.int32, (rows, out.shape[0]), 0)
        row = row + jnp.where(row < half, bases[0], bases[1] - half)
        hot = (row == ids[k : k + 1, :]).astype(jnp.bfloat16)
        dims = (((0,), (0,)), ((), ()))
        out[:, :norb] = lax.dot_general(hot, orb[...], dims, preferred_element_type=jnp.float32).astype(out.dtype)
        picked = [
            lax.dot_general(hot[k * half : (k + 1) * half], tgt[...], dims, preferred_element_type=jnp.float32)
            for k, tgt in enumerate((own_tgt, sib_tgt))
        ]
        out[:, norb:] = (picked[0] + picked[1]).astype(out.dtype)


def pick(table, ids, orb, own_tgt, sib_tgt):
    out = jax.ShapeDtypeStruct((ids.shape[1], orb.shape[1] + own_tgt.shape[1]), orb.dtype)
    whole = pl.BlockSpec(memory_space=pltpu.VMEM)
    return pl.pallas_call(
        pick_kernel,
        out_shape=(out, out),
        in_specs=[pl.BlockSpec(memory_space=pltpu.SMEM)] + [whole] * 4,
        out_specs=(whole, whole),
        compiler_params=pltpu.CompilerParams(vmem_limit_bytes=32 << 20),
        name="pick",
    )(table, ids, orb, own_tgt, sib_tgt)


def apply_parts(slab, parts, potential, table, row_at, col_at, count, total, last=False):
    tile = slab.shape[0] // 2
    norb = slab.shape[1]
    points = sum(p.shape[0] for p in parts) // count
    width = parts[0].shape[1]
    nj = width - norb
    first = total is None

    def body(t, slab_ref, *refs):
        ours, pots = refs[: len(parts)], refs[len(parts) : len(parts) + count]
        here = pl.ds(pl.multiple_of(pl.program_id(0) * tile, tile), tile)
        orb = jnp.concatenate([p[:, :norb] for p in ours], axis=0)
        tgt = jnp.concatenate([p[:, norb:] for p in ours], axis=0)
        products = lax.dot_general(
            slab_ref[here, :], orb, (((1,), (1,)), ((), ())), preferred_element_type=jnp.float32
        )
        pot = jnp.concatenate([p[...] for p in pots], axis=1)
        weighted = (pot.astype(jnp.float32) * products).astype(jnp.bfloat16)
        term = jnp.dot(weighted, tgt, preferred_element_type=jnp.float32)
        if not first:
            term = refs[len(parts) + count][here, :] + term
        if not last:
            refs[-1][here, :] = term
            return
        for k, out in enumerate(refs[-2:]):

            @pl.when(pl.program_id(0) == k)
            def _():
                out[...] = term.astype(out.dtype)

    def pot_spec(k):
        return pl.BlockSpec((tile, points), lambda i, t: (t[row_at + i], t[col_at + k]))

    whole = pl.BlockSpec(memory_space=pltpu.VMEM)
    specs = [whole] * (1 + len(parts)) + [pot_spec(k) for k in range(count)]
    args = [slab, *parts] + [potential] * count
    if not first:
        specs.append(whole)
        args.append(total)
    flops = slab.shape[0] * points * count * width // 2
    halves = tuple(jax.ShapeDtypeStruct((tile, nj), t) for t in (jnp.float32, jnp.bfloat16))
    return pl.pallas_call(
        body,
        out_shape=halves if last else jax.ShapeDtypeStruct((slab.shape[0], nj), jnp.float32),
        grid_spec=pltpu.PrefetchScalarGridSpec(
            num_scalar_prefetch=1, grid=(2,), in_specs=specs, out_specs=(whole,) * 2 if last else whole
        ),
        input_output_aliases={} if first or last else {len(args): 0},
        cost_estimate=pl.CostEstimate(
            flops=flops, bytes_accessed=count * slab.shape[0] * points * 2, transcendentals=0
        ),
        compiler_params=pltpu.CompilerParams(vmem_limit_bytes=15 << 20),
        name="apply",
    )(table, *args)


def local(orbitals, targets, points, potential):
    own_rows = orbitals.shape[0]
    potential = pltpu.with_memory_space_constraint(potential, pltpu.HBM)
    count = points.shape[1]
    y, x, zl, zh, c = (lax.axis_index(a) for a in AXES)
    slab_start = ((y * RING + x) * 2 + zl) * own_rows * 4

    n = lax.iota(jnp.int32, SIDE + 1)
    code = jnp.zeros_like(n)
    for k, (dy, dx) in enumerate(ORDER):
        code = jnp.where(n == k, dy * RING + dx, code)
    cols = (y + code // RING) % RING * RING + (x + code % RING) % RING
    half_at = jnp.where(n < FAR, zh, 1 - zh)
    rows = half_at * 2 + jnp.where((n - NEAR) % 2 == 0, c, 1 - c)
    table = jnp.where(n < NEAR, cols, jnp.where(n < BASE, rows, jnp.where(n < SIDE, slab_start, zl)))
    table = table.astype(jnp.int32)

    sib_orb = take_from(orbitals, "c", 1)
    sib_tgt = take_from(targets, "c", 1)
    far_points = take_from(points, "zh", 1)
    near_slab = jnp.concatenate([orbitals, sib_orb], axis=0)
    ids = jnp.concatenate([points, far_points], axis=0)
    mine, theirs = pick(table, ids, near_slab, targets, sib_tgt)
    block = mine + take_from(theirs, "zh", 1)
    lower = table[SIDE:].reshape(1, 1) == 0

    def in_order(own, other):
        return jnp.concatenate([jnp.where(lower, own, other), jnp.where(lower, other, own)], axis=0)

    def near_apply(parts, ats, total, last=False):
        return apply_parts(near_slab, parts, potential, table, NEAR, ORDER.index(ats[0]), len(ats), total, last)

    def far_apply(parts, ats, total, last=False):
        return apply_parts(far_slab, parts, potential, table, FAR, ORDER.index(ats[0]), len(ats), total, last)

    own = {at: take_from(block, axis, side) for at, axis, side in NEXT}
    other = take_from(block, "zl", 1)
    far_slab = take_from(after(near_slab, *own.values()), "zh", 1)
    pair = {at: in_order(own[at], take_from(other, axis, side)) for at, axis, side in NEXT}
    pair[0, 0] = in_order(block, other)

    def joined(whole, half):
        return jnp.concatenate([pair[whole], half], axis=0)

    from_right = take_from(joined((1, 0), pair[0, 1][:count]), "x", 1)
    from_left = take_from(joined((3, 0), pair[0, 3][count:]), "x", -1)
    from_up = take_from(joined((0, 3), pair[1, 0][:count]), "y", 1)
    from_down = take_from(joined((0, 1), pair[3, 0][count:]), "y", -1)
    first = ((0, 0), *(at for at, _, _ in NEXT))
    near = near_apply([pair[at] for at in first], first, None)
    both = 2 * count
    from_right, from_left, from_up, from_down = (after(v, near) for v in (from_right, from_left, from_up, from_down))
    pair[1, 1], pair[3, 3] = from_right[:both], from_left[:both]
    pair[1, 3], pair[3, 1] = from_up[:both], from_down[:both]
    pair[0, 2] = jnp.concatenate([from_right[both:], from_left[both:]], axis=0)
    pair[2, 0] = jnp.concatenate([from_up[both:], from_down[both:]], axis=0)

    second = ((1, 1), (3, 3), (1, 3), (3, 1), (0, 2), (2, 0))
    third = ((2, 1), (2, 3), (3, 2), (1, 2), (2, 2))
    last = [
        take_from(jnp.concatenate([pair[1, 1], pair[1, 3][:count]], axis=0), "y", 1),
        take_from(jnp.concatenate([pair[3, 3][count:], pair[0, 2]], axis=0), "y", -1),
        take_from(pair[1, 1][:count], "x", 1),
        take_from(pair[1, 3][count:], "x", -1),
        take_from(pair[2, 0], "x", 2),
    ]
    far = far_apply([pair[at] for at in first + second], first + second, None)
    near = near_apply([pair[at] for at in second], second, after(near, far))
    last, far, near = lax.optimization_barrier((last, far, near))
    kept, sent = far_apply(last, third, far, True)
    far = (kept + take_from(sent, "c", 1)).astype(jnp.bfloat16)
    away = take_from(far, "zh", 1)
    kept, sent = near_apply(last, third, after(near, far), True)
    near = kept + take_from(after(sent, away), "c", 1)
    return (-(near + away.astype(jnp.float32))).astype(jnp.bfloat16)


def solution(mesh):
    torus = Mesh(mesh.devices.reshape(RING, RING, 2, 2, 2), AXES)
    placed = (P(AXES, None), P(AXES, None), P(IPTS, SLABS), P(SLABS, IPTS))
    return jax.shard_map(local, mesh=torus, in_specs=placed, out_specs=P(AXES, None), check_vma=False)
```

```python
import jax
import jax.numpy as jnp
from jax import lax
from jax.experimental import pallas as pl
from jax.experimental.pallas import tpu as pltpu
from jax.sharding import Mesh
from jax.sharding import PartitionSpec as P

AXES = ("y", "x", "zl", "zh", "c")
SLABS = ("y", "x", "zl")
IPTS = ("zh", "c")
RING = 4
ORDER = (
    (0, 0), (0, 1), (0, 3), (1, 0), (3, 0), (1, 1), (3, 3), (1, 3), (3, 1), (0, 2), (2, 0),
    (2, 1), (2, 3), (3, 2), (1, 2), (2, 2),
)
NEAR, FAR, BASE, SIDE = 16, 18, 20, 21
NEXT = (((0, 1), "x", 1), ((0, 3), "x", -1), ((1, 0), "y", 1), ((3, 0), "y", -1))


def take_from(value, axis, side):
    n = lax.axis_size(axis)
    return lax.ppermute(value, axis, [((i + side) % n, i) for i in range(n)])


def after(value, *others):
    return lax.optimization_barrier((value, others))[0]


def pick_kernel(table, ids, orb, own_tgt, sib_tgt, mine, theirs):
    rows, norb = orb.shape
    half = rows // 2
    bases = [table[BASE] + table[NEAR + k] * half for k in range(2)]
    for k, out in ((0, mine), (1, theirs)):
        row = lax.broadcasted_iota(jnp.int32, (rows, out.shape[0]), 0)
        row = row + jnp.where(row < half, bases[0], bases[1] - half)
        hot = (row == ids[k : k + 1, :]).astype(jnp.bfloat16)
        dims = (((0,), (0,)), ((), ()))
        out[:, :norb] = lax.dot_general(hot, orb[...], dims, preferred_element_type=jnp.float32).astype(out.dtype)
        picked = [
            lax.dot_general(hot[k * half : (k + 1) * half], tgt[...], dims, preferred_element_type=jnp.float32)
            for k, tgt in enumerate((own_tgt, sib_tgt))
        ]
        out[:, norb:] = (picked[0] + picked[1]).astype(out.dtype)


def pick(table, ids, orb, own_tgt, sib_tgt):
    out = jax.ShapeDtypeStruct((ids.shape[1], orb.shape[1] + own_tgt.shape[1]), orb.dtype)
    whole = pl.BlockSpec(memory_space=pltpu.VMEM)
    return pl.pallas_call(
        pick_kernel,
        out_shape=(out, out),
        in_specs=[pl.BlockSpec(memory_space=pltpu.SMEM)] + [whole] * 4,
        out_specs=(whole, whole),
        compiler_params=pltpu.CompilerParams(vmem_limit_bytes=32 << 20),
        name="pick",
    )(table, ids, orb, own_tgt, sib_tgt)


def apply_parts(slab, parts, potential, table, row_at, col_at, count, total, last=False):
    tile = slab.shape[0] // 2
    norb = slab.shape[1]
    points = sum(p.shape[0] for p in parts) // count
    width = parts[0].shape[1]
    nj = width - norb
    first = total is None

    def body(t, slab_ref, *refs):
        ours, pots = refs[: len(parts)], refs[len(parts) : len(parts) + count]
        here = pl.ds(pl.multiple_of(pl.program_id(0) * tile, tile), tile)
        orb = jnp.concatenate([p[:, :norb] for p in ours], axis=0)
        tgt = jnp.concatenate([p[:, norb:] for p in ours], axis=0)
        products = lax.dot_general(
            slab_ref[here, :], orb, (((1,), (1,)), ((), ())), preferred_element_type=jnp.float32
        )
        pot = jnp.concatenate([p[...] for p in pots], axis=1)
        weighted = (pot.astype(jnp.float32) * products).astype(jnp.bfloat16)
        term = jnp.dot(weighted, tgt, preferred_element_type=jnp.float32)
        if not first:
            term = refs[len(parts) + count][here, :] + term
        if not last:
            refs[-1][here, :] = term
            return
        for k, out in enumerate(refs[-2:]):

            @pl.when(pl.program_id(0) == k)
            def _():
                out[...] = term.astype(out.dtype)

    def pot_spec(k):
        return pl.BlockSpec((tile, points), lambda i, t: (t[row_at + i], t[col_at + k]))

    whole = pl.BlockSpec(memory_space=pltpu.VMEM)
    specs = [whole] * (1 + len(parts)) + [pot_spec(k) for k in range(count)]
    args = [slab, *parts] + [potential] * count
    if not first:
        specs.append(whole)
        args.append(total)
    flops = slab.shape[0] * points * count * width // 2
    halves = tuple(jax.ShapeDtypeStruct((tile, nj), t) for t in (jnp.float32, jnp.bfloat16))
    return pl.pallas_call(
        body,
        out_shape=halves if last else jax.ShapeDtypeStruct((slab.shape[0], nj), jnp.float32),
        grid_spec=pltpu.PrefetchScalarGridSpec(
            num_scalar_prefetch=1, grid=(2,), in_specs=specs, out_specs=(whole,) * 2 if last else whole
        ),
        input_output_aliases={} if first or last else {len(args): 0},
        cost_estimate=pl.CostEstimate(
            flops=flops, bytes_accessed=count * slab.shape[0] * points * 2, transcendentals=0
        ),
        compiler_params=pltpu.CompilerParams(vmem_limit_bytes=15 << 20),
        name="apply",
    )(table, *args)


def local(orbitals, targets, points, potential):
    own_rows = orbitals.shape[0]
    potential = pltpu.with_memory_space_constraint(potential, pltpu.HBM)
    count = points.shape[1]
    y, x, zl, zh, c = (lax.axis_index(a) for a in AXES)
    slab_start = ((y * RING + x) * 2 + zl) * own_rows * 4

    n = lax.iota(jnp.int32, SIDE + 1)
    code = jnp.zeros_like(n)
    for k, (dy, dx) in enumerate(ORDER):
        code = jnp.where(n == k, dy * RING + dx, code)
    cols = (y + code // RING) % RING * RING + (x + code % RING) % RING
    half_at = jnp.where(n < FAR, zh, 1 - zh)
    rows = half_at * 2 + jnp.where((n - NEAR) % 2 == 0, c, 1 - c)
    table = jnp.where(n < NEAR, cols, jnp.where(n < BASE, rows, jnp.where(n < SIDE, slab_start, zl)))
    table = table.astype(jnp.int32)

    sib_orb = take_from(orbitals, "c", 1)
    sib_tgt = take_from(targets, "c", 1)
    far_points = take_from(points, "zh", 1)
    near_slab = jnp.concatenate([orbitals, sib_orb], axis=0)
    ids = jnp.concatenate([points, far_points], axis=0)
    mine, theirs = pick(table, ids, near_slab, targets, sib_tgt)
    block = mine + take_from(theirs, "zh", 1)
    lower = table[SIDE:].reshape(1, 1) == 0

    def in_order(own, other):
        return jnp.concatenate([jnp.where(lower, own, other), jnp.where(lower, other, own)], axis=0)

    def near_apply(parts, ats, total, last=False):
        return apply_parts(near_slab, parts, potential, table, NEAR, ORDER.index(ats[0]), len(ats), total, last)

    def far_apply(parts, ats, total, last=False):
        return apply_parts(far_slab, parts, potential, table, FAR, ORDER.index(ats[0]), len(ats), total, last)

    own = {at: take_from(block, axis, side) for at, axis, side in NEXT}
    other = take_from(block, "zl", 1)
    far_slab = take_from(after(near_slab, *own.values()), "zh", 1)
    pair = {at: in_order(own[at], take_from(other, axis, side)) for at, axis, side in NEXT}
    pair[0, 0] = in_order(block, other)

    def joined(whole, half):
        return jnp.concatenate([pair[whole], half], axis=0)

    from_right = take_from(joined((1, 0), pair[0, 1][:count]), "x", 1)
    from_left = take_from(joined((3, 0), pair[0, 3][count:]), "x", -1)
    from_up = take_from(joined((0, 3), pair[1, 0][:count]), "y", 1)
    from_down = take_from(joined((0, 1), pair[3, 0][count:]), "y", -1)
    first = ((0, 0), *(at for at, _, _ in NEXT))
    near = near_apply([pair[at] for at in first], first, None)
    both = 2 * count
    from_right, from_left, from_up, from_down = (after(v, near) for v in (from_right, from_left, from_up, from_down))
    pair[1, 1], pair[3, 3] = from_right[:both], from_left[:both]
    pair[1, 3], pair[3, 1] = from_up[:both], from_down[:both]
    pair[0, 2] = jnp.concatenate([from_right[both:], from_left[both:]], axis=0)
    pair[2, 0] = jnp.concatenate([from_up[both:], from_down[both:]], axis=0)

    second = ((1, 1), (3, 3), (1, 3), (3, 1), (0, 2), (2, 0))
    third = ((2, 1), (2, 3), (3, 2), (1, 2), (2, 2))
    last = [
        take_from(jnp.concatenate([pair[1, 1], pair[1, 3][:count]], axis=0), "y", 1),
        take_from(jnp.concatenate([pair[3, 3][count:], pair[0, 2]], axis=0), "y", -1),
        take_from(pair[1, 1][:count], "x", 1),
        take_from(pair[1, 3][count:], "x", -1),
        take_from(pair[2, 0], "x", 2),
    ]
    far = far_apply([pair[at] for at in first + second], first + second, None)
    near = near_apply([pair[at] for at in second], second, after(near, far))
    last, far, near = lax.optimization_barrier((last, far, near))
    kept, sent = far_apply(last, third, far, True)
    far = (kept + take_from(sent, "c", 1)).astype(jnp.bfloat16)
    away = take_from(jnp.concatenate([far, far[:16]], axis=0), "zh", 1)[:own_rows]
    kept, sent = near_apply(last, third, after(near, far), True)
    near = kept + take_from(sent, "c", 1)
    return (-(near + away.astype(jnp.float32))).astype(jnp.bfloat16)


def solution(mesh):
    torus = Mesh(mesh.devices.reshape(RING, RING, 2, 2, 2), AXES)
    placed = (P(AXES, None), P(AXES, None), P(IPTS, SLABS), P(SLABS, IPTS))
    return jax.shard_map(local, mesh=torus, in_specs=placed, out_specs=P(AXES, None), check_vma=False)
```

```python
import jax
import jax.numpy as jnp
from jax import lax
from jax.experimental import pallas as pl
from jax.experimental.pallas import tpu as pltpu
from jax.sharding import Mesh
from jax.sharding import PartitionSpec as P

AXES = ("y", "x", "zl", "zh", "c")
SLABS = ("y", "x", "zl")
IPTS = ("zh", "c")
RING = 4
ORDER = (
    (0, 0), (0, 1), (0, 3), (1, 0), (3, 0), (1, 1), (3, 3), (1, 3), (3, 1), (0, 2), (2, 0),
    (2, 1), (2, 3), (3, 2), (1, 2), (2, 2),
)
NEAR, FAR, BASE, SIDE = 16, 18, 20, 21
NEXT = (((0, 1), "x", 1), ((0, 3), "x", -1), ((1, 0), "y", 1), ((3, 0), "y", -1))


def take_from(value, axis, side):
    n = lax.axis_size(axis)
    return lax.ppermute(value, axis, [((i + side) % n, i) for i in range(n)])


def after(value, *others):
    return lax.optimization_barrier((value, others))[0]


def pick_kernel(table, ids, orb, own_tgt, sib_tgt, mine, theirs):
    rows, norb = orb.shape
    half = rows // 2
    bases = [table[BASE] + table[NEAR + k] * half for k in range(2)]
    for k, out in ((0, mine), (1, theirs)):
        row = lax.broadcasted_iota(jnp.int32, (rows, out.shape[0]), 0)
        row = row + jnp.where(row < half, bases[0], bases[1] - half)
        hot = (row == ids[k : k + 1, :]).astype(jnp.bfloat16)
        dims = (((0,), (0,)), ((), ()))
        out[:, :norb] = lax.dot_general(hot, orb[...], dims, preferred_element_type=jnp.float32).astype(out.dtype)
        picked = [
            lax.dot_general(hot[k * half : (k + 1) * half], tgt[...], dims, preferred_element_type=jnp.float32)
            for k, tgt in enumerate((own_tgt, sib_tgt))
        ]
        out[:, norb:] = (picked[0] + picked[1]).astype(out.dtype)


def pick(table, ids, orb, own_tgt, sib_tgt):
    out = jax.ShapeDtypeStruct((ids.shape[1], orb.shape[1] + own_tgt.shape[1]), orb.dtype)
    whole = pl.BlockSpec(memory_space=pltpu.VMEM)
    return pl.pallas_call(
        pick_kernel,
        out_shape=(out, out),
        in_specs=[pl.BlockSpec(memory_space=pltpu.SMEM)] + [whole] * 4,
        out_specs=(whole, whole),
        compiler_params=pltpu.CompilerParams(vmem_limit_bytes=32 << 20),
        name="pick",
    )(table, ids, orb, own_tgt, sib_tgt)


def apply_parts(slab, parts, potential, table, row_at, col_at, count, total, last=False):
    tile = slab.shape[0] // 2
    norb = slab.shape[1]
    points = sum(p.shape[0] for p in parts) // count
    width = parts[0].shape[1]
    nj = width - norb
    first = total is None

    def body(t, slab_ref, *refs):
        ours, pots = refs[: len(parts)], refs[len(parts) : len(parts) + count]
        here = pl.ds(pl.multiple_of(pl.program_id(0) * tile, tile), tile)
        orb = jnp.concatenate([p[:, :norb] for p in ours], axis=0)
        tgt = jnp.concatenate([p[:, norb:] for p in ours], axis=0)
        products = lax.dot_general(
            slab_ref[here, :], orb, (((1,), (1,)), ((), ())), preferred_element_type=jnp.float32
        )
        pot = jnp.concatenate([p[...] for p in pots], axis=1)
        weighted = (pot.astype(jnp.float32) * products).astype(jnp.bfloat16)
        term = jnp.dot(weighted, tgt, preferred_element_type=jnp.float32)
        if not first:
            term = refs[len(parts) + count][here, :] + term
        if not last:
            refs[-1][here, :] = term
            return
        for k, out in enumerate(refs[-2:]):

            @pl.when(pl.program_id(0) == k)
            def _():
                out[...] = term.astype(out.dtype)

    def pot_spec(k):
        return pl.BlockSpec((tile, points), lambda i, t: (t[row_at + i], t[col_at + k]))

    whole = pl.BlockSpec(memory_space=pltpu.VMEM)
    specs = [whole] * (1 + len(parts)) + [pot_spec(k) for k in range(count)]
    args = [slab, *parts] + [potential] * count
    if not first:
        specs.append(whole)
        args.append(total)
    flops = slab.shape[0] * points * count * width // 2
    halves = tuple(jax.ShapeDtypeStruct((tile, nj), t) for t in (jnp.float32, jnp.bfloat16))
    return pl.pallas_call(
        body,
        out_shape=halves if last else jax.ShapeDtypeStruct((slab.shape[0], nj), jnp.float32),
        grid_spec=pltpu.PrefetchScalarGridSpec(
            num_scalar_prefetch=1, grid=(2,), in_specs=specs, out_specs=(whole,) * 2 if last else whole
        ),
        input_output_aliases={} if first or last else {len(args): 0},
        cost_estimate=pl.CostEstimate(
            flops=flops, bytes_accessed=count * slab.shape[0] * points * 2, transcendentals=0
        ),
        compiler_params=pltpu.CompilerParams(vmem_limit_bytes=15 << 20),
        name="apply",
    )(table, *args)


def local(orbitals, targets, points, potential):
    own_rows = orbitals.shape[0]
    potential = pltpu.with_memory_space_constraint(potential, pltpu.HBM)
    count = points.shape[1]
    y, x, zl, zh, c = (lax.axis_index(a) for a in AXES)
    slab_start = ((y * RING + x) * 2 + zl) * own_rows * 4

    n = lax.iota(jnp.int32, SIDE + 1)
    code = jnp.zeros_like(n)
    for k, (dy, dx) in enumerate(ORDER):
        code = jnp.where(n == k, dy * RING + dx, code)
    cols = (y + code // RING) % RING * RING + (x + code % RING) % RING
    half_at = jnp.where(n < FAR, zh, 1 - zh)
    rows = half_at * 2 + jnp.where((n - NEAR) % 2 == 0, c, 1 - c)
    table = jnp.where(n < NEAR, cols, jnp.where(n < BASE, rows, jnp.where(n < SIDE, slab_start, zl)))
    table = table.astype(jnp.int32)

    sib_orb = take_from(orbitals, "c", 1)
    sib_tgt = take_from(targets, "c", 1)
    far_points = take_from(points, "zh", 1)
    near_slab = jnp.concatenate([orbitals, sib_orb], axis=0)
    ids = jnp.concatenate([points, far_points], axis=0)
    mine, theirs = pick(table, ids, near_slab, targets, sib_tgt)
    block = mine + take_from(theirs, "zh", 1)
    lower = table[SIDE:].reshape(1, 1) == 0

    def in_order(own, other):
        return jnp.concatenate([jnp.where(lower, own, other), jnp.where(lower, other, own)], axis=0)

    def near_apply(parts, ats, total, last=False):
        return apply_parts(near_slab, parts, potential, table, NEAR, ORDER.index(ats[0]), len(ats), total, last)

    def far_apply(parts, ats, total, last=False):
        return apply_parts(far_slab, parts, potential, table, FAR, ORDER.index(ats[0]), len(ats), total, last)

    own = {at: take_from(block, axis, side) for at, axis, side in NEXT}
    other = take_from(block, "zl", 1)
    far_slab = take_from(after(near_slab, *own.values()), "zh", 1)
    pair = {at: in_order(own[at], take_from(other, axis, side)) for at, axis, side in NEXT}
    pair[0, 0] = in_order(block, other)

    def joined(whole, half):
        return jnp.concatenate([pair[whole], half], axis=0)

    from_right = take_from(joined((1, 0), pair[0, 1][:count]), "x", 1)
    from_left = take_from(joined((3, 0), pair[0, 3][count:]), "x", -1)
    from_up = take_from(joined((0, 3), pair[1, 0][:count]), "y", 1)
    from_down = take_from(joined((0, 1), pair[3, 0][count:]), "y", -1)
    first = ((0, 0), *(at for at, _, _ in NEXT))
    near = near_apply([pair[at] for at in first], first, None)
    both = 2 * count
    from_right, from_left = after(from_right, near), after(from_left, near)
    pair[1, 1], pair[3, 3] = from_right[:both], from_left[:both]
    pair[1, 3], pair[3, 1] = from_up[:both], from_down[:both]
    pair[0, 2] = jnp.concatenate([from_right[both:], from_left[both:]], axis=0)
    pair[2, 0] = jnp.concatenate([from_up[both:], from_down[both:]], axis=0)

    second = ((1, 1), (3, 3), (1, 3), (3, 1), (0, 2), (2, 0))
    third = ((2, 1), (2, 3), (3, 2), (1, 2), (2, 2))
    last = [
        take_from(jnp.concatenate([pair[1, 1], pair[1, 3][:count]], axis=0), "y", 1),
        take_from(jnp.concatenate([pair[3, 3][count:], pair[0, 2]], axis=0), "y", -1),
        take_from(pair[1, 1][:count], "x", 1),
        take_from(pair[1, 3][count:], "x", -1),
        take_from(pair[2, 0], "x", 2),
    ]
    far = far_apply([pair[at] for at in first + second], first + second, None)
    near = near_apply([pair[at] for at in second], second, after(near, far))
    last, far, near = lax.optimization_barrier((last, far, near))
    kept, sent = far_apply(last, third, far, True)
    far = (kept + take_from(sent, "c", 1)).astype(jnp.bfloat16)
    away = take_from(jnp.concatenate([far, far[:16]], axis=0), "zh", 1)[:own_rows]
    kept, sent = near_apply(last, third, after(near, far), True)
    near = kept + take_from(sent, "c", 1)
    return (-(near + away.astype(jnp.float32))).astype(jnp.bfloat16)


def solution(mesh):
    torus = Mesh(mesh.devices.reshape(RING, RING, 2, 2, 2), AXES)
    placed = (P(AXES, None), P(AXES, None), P(IPTS, SLABS), P(SLABS, IPTS))
    return jax.shard_map(local, mesh=torus, in_specs=placed, out_specs=P(AXES, None), check_vma=False)
```
